32 devices in a mesh: expert: 32 (over z, y, x, core).
Axes of the slice: x: 2, y: 2, z: 4, core: 2. Of those that a mesh axis runs over, the one named last changes fastest.
Arguments:
- tokens: bfloat16 [4096, 3584], P('expert'), may hold values from -6 to 6
- cotangent: bfloat16 [4096, 3584], P('expert'), may hold values from -6 to 6
- routes: int32 [4096, 8], P('expert'), may hold values from 0 to 15, all different within a row; in each aligned block of 128 rows (0 to 127, 128 to 255, ...) at most 80 rows name the same one
- gates: bfloat16 [4096, 8], P('expert'), may hold values from 0.049804688 to 0.29882812
- previous_row: int32 [16], replicated, may hold values from 0 to 15, each once
- gu_payload: bfloat16 [16, 3584, 2048], P(None, 'expert'), may hold values from -0.09375 to 0.09375
- gu_scales: float32 [16, 28, 16], replicated, may hold values from 0.5 to 2
- down_payload: bfloat16 [16, 1024, 3584], P(None, 'expert'), may hold values from -0.1875 to 0.1875
- down_scales: float32 [16, 8, 28], replicated, may hold values from 0.5 to 2
Outputs:
- layer_out: bfloat16 [4096, 3584], P('expert')
- gate_grad: float32 [4096, 8], P('expert')
The draws below stay inside these ranges and needn't reach their ends.
Inputs may be any that keep to these rules, and one draw needn't show every extreme that they name: `routes`: each token names 8 different experts; among the tokens of one device no expert is named by more than 80 of them, and in some devices' tokens one expert is named by exactly 80. `previous_row`: each stored row holds exactly one expert.
All inputs are finite; a program needn't handle non-finite values.
Results may differ from the reference program's by a relative error of at most 0.0076.
Values may be sent and summed in bfloat16 or wider, within the bound.
A program may use at most 256 MiB of HBM per device.

```python
import math
import jax
import jax.numpy as jnp
import numpy as np
from jax import lax

D = 3584
FF = 1024
TOP = 8
TOK_DEV = 128
SLOTS = 32
EXPERTS = 16
MOST = 80
TOKENS = 4096


def steps_of(key, shape, cuts, smallest, largest):
    level, own = 1.0, jax.random.fold_in(key, 6)
    for axis_at, blocks in cuts:
        heights = jnp.exp(jax.random.uniform(jax.random.fold_in(own, axis_at), (blocks,), jnp.float32, smallest / len(cuts), largest / len(cuts)))
        level = level * jnp.repeat(heights, shape[axis_at] // blocks).reshape([-1 if axis == axis_at else 1 for axis in range(len(shape))])
    return level


def deal_out(own_key, own, number, rows, amount, top, limit, skew):
    sequence = jax.random.permutation(own_key, amount)
    heavy_load, ordinary = shares(amount, rows * top, limit, skew, True), shares(amount, rows * top, limit, skew, False)
    places = jnp.arange(amount)

    def named(lengths, rotation):
        used = int((lengths > 0).sum())
        fixed = max(1, used // 4)
        shifted = fixed + (places - fixed + rotation * (used - fixed)) % max(1, amount - fixed)
        return jnp.zeros((amount,), jnp.int32).at[sequence[jnp.where(places < fixed, places, shifted)]].set(jnp.asarray(lengths, jnp.int32))

    lengths = jnp.where(number % 4 == 0, named(heavy_load, number // 4), named(ordinary, number - number // 4 - 1))
    mixed = jax.random.permutation(jax.random.fold_in(own, 3), amount)
    source_of, sink = mixed[0:amount // 2 * 2:2], mixed[1:amount // 2 * 2:2]
    room = jnp.minimum(lengths[source_of] - 1, limit - lengths[sink]) // 2
    room = jnp.where((source_of == sequence[0]) | (sink == sequence[0]) | (lengths[sink] == 0), 0, jnp.maximum(room, 0))
    shifted = jax.random.randint(jax.random.fold_in(own, 4), (amount // 2,), 0, 1 << 20) % (room + 1)
    lengths = lengths.at[source_of].add(-shifted).at[sink].add(shifted)
    labels = jnp.searchsorted(jnp.cumsum(lengths), jnp.arange(rows * top), side="right").astype(jnp.int32)
    grid = labels.reshape(top, rows).T
    grid = grid[jax.random.permutation(jax.random.fold_in(own, 1), rows)]
    rotation = jax.random.randint(jax.random.fold_in(own, 2), (rows, 1), 0, top)
    return jnp.take_along_axis(grid, (jnp.arange(top)[None, :] + rotation) % top, axis=1)


def shares(amount, total, most, skew, full):
    weights = [(1 << 20) // math.isqrt(standing ** skew) + 1 for standing in range(1, amount + 1)]
    largest = most if full else min(most, max(-(-total // amount), total * weights[0] // sum(weights)))
    least = 1 if total - largest >= amount - 1 else 0
    holding, spare = [largest] + [least] * (amount - 1), total - largest - least * (amount - 1)
    while spare > 0:
        free = [i for i in range(1, amount) if holding[i] < largest] or [i for i in range(1, amount) if holding[i] < most]
        whole, left = sum([weights[i] for i in free]), spare
        for i in free:
            more = min(most - holding[i], max(1, left * weights[i] // whole), spare)
            holding[i] = holding[i] + more
            spare = spare - more
    return np.array(holding)


def normal_values(own_key, shape, spread, bound, cuts=(), held_as=jnp.bfloat16):
    values = spread * jax.random.normal(own_key, shape, jnp.float32)
    if cuts:
        values = values * steps_of(own_key, shape, cuts, -0.22, 0.18)
    return jnp.clip(values, -bound, bound).astype(held_as)


def setup_inputs(seed: int = 0) -> dict:
    seeds = jax.random.split(jax.random.key(seed), 10)
    tokens = normal_values(seeds[0], (TOKENS, D), 1.0, 6.0, ((0, 32),))
    cotangent = normal_values(seeds[1], (TOKENS, D), 1.0, 6.0, ((0, 32),))
    routes_keys = jax.random.split(jax.random.fold_in(seeds[2], 1), TOKENS // TOK_DEV)
    routes_turns = jax.random.permutation(jax.random.fold_in(seeds[2], 3), TOKENS // TOK_DEV)
    routes = jax.vmap(lambda own, number: deal_out(jax.random.fold_in(seeds[2], 2), own, number, TOK_DEV, EXPERTS, TOP, MOST, 2))(routes_keys, routes_turns).reshape((TOKENS, TOP))
    gates = jnp.clip(0.049804688 + 0.24902344 * jax.random.uniform(seeds[3], (TOKENS, TOP), jnp.float32) ** steps_of(seeds[3], (TOKENS, TOP), ((0, 32),), -0.2, 0.2), 0.049804688, 0.29882812).astype(jnp.bfloat16)
    previous_row = jax.random.permutation(seeds[4], EXPERTS).astype(jnp.int32)
    gu_payload = normal_values(seeds[5], (EXPERTS, D, 2 * FF), D ** -0.5, 0.09375, ((1, 32),))
    gu_scales = jnp.clip(jnp.exp(jax.random.uniform(seeds[6], (EXPERTS, D // 128, 2 * FF // 128), jnp.float32, math.log(0.5), math.log(2.0))), 0.5, 2.0)
    down_payload = normal_values(seeds[7], (EXPERTS, FF, D), FF ** -0.5, 0.1875, ((1, 32),))
    down_scales = jnp.clip(jnp.exp(jax.random.uniform(seeds[8], (EXPERTS, FF // 128, D // 128), jnp.float32, math.log(0.5), math.log(2.0))), 0.5, 2.0)
    return {"tokens": tokens, "cotangent": cotangent, "routes": routes, "gates": gates, "previous_row": previous_row, "gu_payload": gu_payload, "gu_scales": gu_scales, "down_payload": down_payload, "down_scales": down_scales}


def dequantize(payload, scales):
    expanded = jnp.repeat(jnp.repeat(scales, 128, axis=0), 128, axis=1)
    return (payload.astype(jnp.float32) * expanded).astype(jnp.bfloat16)


def reference(tokens, cotangent, routes, gates, previous_row, gu_payload, gu_scales, down_payload, down_scales):
    flat_routes = routes.reshape(-1)
    route_count = flat_routes.shape[0]
    row_limit = MOST * SLOTS
    token_of = jnp.arange(route_count, dtype=jnp.int32) // TOP
    route_ids = jnp.arange(route_count, dtype=jnp.int32)

    def one_expert(gathered, expert):
        is_match = (flat_routes == expert).astype(jnp.int32)
        route_rank = jnp.cumsum(is_match) - 1
        target = jnp.where(is_match == 1, route_rank, row_limit).astype(jnp.int32)
        token_table = jnp.zeros((row_limit,), jnp.int32).at[target].set(token_of, mode="drop")
        route_table = jnp.full((row_limit,), route_count, jnp.int32).at[target].set(route_ids, mode="drop")
        stored = previous_row[expert]
        w_gu = dequantize(gu_payload[stored], gu_scales[stored])
        w_down = dequantize(down_payload[stored], down_scales[stored])
        hidden = jnp.dot(tokens[token_table], w_gu, preferred_element_type=jnp.float32)
        active = (jax.nn.silu(hidden[:, :FF]) * hidden[:, FF:]).astype(jnp.bfloat16)
        result = jnp.dot(active, w_down, preferred_element_type=jnp.float32).astype(jnp.bfloat16)
        return gathered.at[route_table].set(result, mode="drop"), None

    start = jnp.zeros((route_count, D), jnp.bfloat16)
    per_route, unused = lax.scan(one_expert, start, jnp.arange(EXPERTS, dtype=jnp.int32))
    stacked = per_route.reshape(-1, TOP, D).astype(jnp.float32)
    layer_out = jnp.einsum("tk,tkd->td", gates.astype(jnp.float32), stacked).astype(jnp.bfloat16)
    gate_grad = jnp.einsum("td,tkd->tk", cotangent.astype(jnp.float32), stacked)
    return layer_out, gate_grad
```

```python
import functools

import jax
import jax.numpy as jnp
from jax import lax
from jax.experimental import pallas as pl
from jax.experimental.pallas import tpu as pltpu
from jax.sharding import PartitionSpec as P


def dequantize(payload, scales):
    expanded = jnp.repeat(jnp.repeat(scales, 128, axis=0), 128, axis=1)
    return (payload.astype(jnp.float32) * expanded).astype(jnp.bfloat16)


def plan(routes, gates, previous_row, most):
    local_count = routes.shape[0]
    rows = previous_row.shape[0]
    ids = jnp.arange(rows, dtype=jnp.int32)
    row_of = jnp.sum(jnp.where(routes[:, :, None] == ids, previous_row, 0), axis=2)
    hits = row_of[:, :, None] == ids
    chosen = jnp.sum(hits.astype(jnp.float32), axis=1)
    gate_of = jnp.sum(jnp.where(hits, gates.astype(jnp.float32)[:, :, None], 0.0), axis=1)
    places = jnp.arange(local_count, dtype=jnp.int32)
    before = (places[:, None] < places[None, :]).astype(jnp.bfloat16)
    rank = jnp.einsum(
        "ut,us->st", before, chosen.astype(jnp.bfloat16), preferred_element_type=jnp.float32
    ).astype(jnp.int32)
    slots = jnp.arange(most, dtype=jnp.int32)
    picked = (rank[:, None, :] == slots[None, :, None]) & (chosen.T[:, None, :] > 0)
    select = picked.astype(jnp.bfloat16)
    weigh = jnp.where(picked, gate_of.T[:, None, :], 0.0).astype(jnp.bfloat16)
    return hits, select.reshape(rows * most, local_count), weigh.reshape(rows * most, local_count)


def shards(
    tokens, cotangent, routes, gates, previous_row, gu_payload, gu_scales, down_payload, down_scales
):
    local_count, model_width = tokens.shape
    top = routes.shape[1]
    hidden_width = gu_payload.shape[2] // 2
    devices = lax.axis_size("expert")
    device_id = lax.axis_index("expert")
    experts = previous_row.shape[0]
    copies = devices // experts
    groups = [[c * experts + i for i in range(experts)] for c in range(copies)]
    most = local_count * top * 5 // (4 * experts)
    hits, select, weigh = plan(routes, gates, previous_row, most)
    outgoing = jnp.dot(select, tokens, preferred_element_type=jnp.float32).astype(jnp.bfloat16)
    outgoing = outgoing.reshape(experts, most, model_width)
    arrived = lax.all_to_all(
        outgoing, "expert", split_axis=0, concat_axis=0, tiled=True, axis_index_groups=groups
    )
    send_gate = jnp.concatenate([gu_payload] * copies, axis=0)
    send_down = jnp.concatenate([down_payload] * copies, axis=0)
    got_gate = lax.all_to_all(send_gate, "expert", split_axis=0, concat_axis=0, tiled=True)
    got_down = lax.all_to_all(send_down, "expert", split_axis=0, concat_axis=0, tiled=True)
    own_row = device_id % experts
    w_gu = dequantize(got_gate.reshape(model_width, 2 * hidden_width), gu_scales[own_row])
    w_down = dequantize(got_down.reshape(hidden_width, model_width), down_scales[own_row])
    row_block = arrived.reshape(-1, model_width)
    hidden = jnp.dot(row_block, w_gu, preferred_element_type=jnp.float32)
    active = (jax.nn.silu(hidden[:, :hidden_width]) * hidden[:, hidden_width:]).astype(jnp.bfloat16)
    result = jnp.dot(active, w_down, preferred_element_type=jnp.float32).astype(jnp.bfloat16)
    returned = lax.all_to_all(
        result.reshape(arrived.shape),
        "expert",
        split_axis=0,
        concat_axis=0,
        tiled=True,
        axis_index_groups=groups,
    ).reshape(-1, model_width)
    layer_out = jnp.einsum(
        "st,sd->td", weigh, returned, preferred_element_type=jnp.float32
    ).astype(jnp.bfloat16)
    dots = jnp.einsum("sd,td->st", returned, cotangent, preferred_element_type=jnp.float32)
    dots = jnp.sum(
        jnp.where(select > 0, dots, 0.0).reshape(experts, most, local_count), axis=1
    )
    gate_grad = jnp.sum(jnp.where(hits, dots.T[:, None, :], 0.0), axis=2)
    return (layer_out, gate_grad)


LANES = 128
PAIR = 2
RING = 4
TILE = 512
MESH = pl.DeviceIdType.MESH


def fits(devices, experts, stored_rows, hidden_rows, hidden_width):
    outer = hidden_width // LANES
    return (
        hidden_width % LANES == 0
        and outer % 2 == 0
        and devices % (2 * outer) == 0
        and experts % PAIR == 0
        and experts <= LANES
        and stored_rows % 16 == 0
        and stored_rows <= LANES
        and hidden_rows % 16 == 0
        and LANES % hidden_rows == 0
    )


def layer_kernel(
    sizes, wgu, wdn, tok, cot,
    out, grads, gu, dn,
    tok_v, cot_v, acc, act, gu_v, dn_v, own_v, y_in, z_in, part, part_out, part_in,
    a2a_s, a2a_r, x_s, x_r, p_s, p_r, own_sem, load_sem, dn_sem, dn_xs, dn_xr, dn_ps, dn_pr,
    tok_s, tok_z, tok_y, loc_sem, ry_s, ry_r, rz_s, rz_r, gr_s, gr_r,
):
    outer, inner, count, rows, width = sizes
    chips, depth = inner // 2, outer // 2
    experts = wdn.shape[0]
    hidden = wdn.shape[1]
    chunks = experts // PAIR
    devices = outer * inner
    me = lax.axis_index("expert")
    o, i = me // inner, me % inner
    zz, yy, xx, c = o // 2, o % 2, i // 2, i % 2
    place = o * chips + xx
    partner = o * inner + xx * 2 + (1 - c)
    y_peer = (zz * 2 + (1 - yy)) * inner + i
    right, left = me + 2 * inner, me - 2 * inner

    def group_peer(r):
        return ((o + r) % outer) * inner + i

    def x_peer(k):
        return o * inner + ((xx + k) % chips) * 2 + c

    def remote(src, dst, send, recv, device):
        return pltpu.make_async_remote_copy(
            src_ref=src, dst_ref=dst, send_sem=send, recv_sem=recv,
            device_id=(device,), device_id_type=MESH,
        )

    def settle(ref, sem):
        pltpu.make_async_copy(ref, ref, sem).wait()

    stage_in = pltpu.make_async_copy(wgu.at[o], own_v, own_sem)
    stage_in.start()
    own_rows = pl.ds(pl.multiple_of(o * count, count), count)
    for source, target, slot in ((tok, tok_v, 0), (cot, cot_v, 1)):
        pltpu.make_async_copy(source, target.at[own_rows], loc_sem.at[slot]).start()

    barrier = pltpu.get_barrier_semaphore()
    for r in range(1, outer):
        pl.semaphore_signal(barrier, inc=1, device_id=(group_peer(r),), device_id_type=MESH)
    for k in range(1, chips):
        pl.semaphore_signal(barrier, inc=1, device_id=(x_peer(k),), device_id_type=MESH)
    pl.semaphore_signal(barrier, inc=1, device_id=(partner,), device_id_type=MESH)
    pl.semaphore_wait(barrier, outer + chips - 1)

    def block(ref, index):
        return ref.at[pl.ds(pl.multiple_of(index * count, count), count)]

    def spread(ref, array, line, direction, source=None):
        target = (right, left, y_peer)[direction]
        there = block(ref, line * 2 + yy)
        arrive = tok_y.at[array, line] if direction == 2 else tok_z.at[array, line]
        return remote(
            there if source is None else source, there,
            tok_s.at[array, direction, line], arrive, target,
        )

    arrays = ((tok_v, 0, tok), (cot_v, 1, cot))
    for ref, array, source in arrays:
        @pl.when(zz < depth - 1)
        def _(ref=ref, array=array, source=source):
            spread(ref, array, zz, 0, source).start()

        @pl.when(zz > 0)
        def _(ref=ref, array=array, source=source):
            spread(ref, array, zz, 1, source).start()

        spread(ref, array, zz, 2, source).start()

    for k in range(1, chips):
        remote(wdn, dn.at[:, i], dn_xs.at[k], dn_xr.at[k], x_peer(k)).start()
    remote(wdn, dn.at[:, i], dn_ps.at[0], dn_pr.at[0], partner).start()

    stage_in.wait()
    stage_out = pltpu.make_async_copy(own_v, gu.at[:, place, c], own_sem)
    stage_out.start()

    def exchange(q):
        for r in range(1, outer):
            remote(
                wgu.at[(o + r) % outer, pl.ds(q * PAIR, PAIR)],
                gu.at[pl.ds(q * PAIR, PAIR), place, c],
                a2a_s, a2a_r.at[q, r], group_peer(r),
            ).start()

    def relay(ref, array, step):
        @pl.when(zz >= step)
        def _():
            line = zz - step
            settle(block(ref, line * 2 + yy), tok_z.at[array, line])

            @pl.when(zz < depth - 1)
            def _():
                spread(ref, array, line, 0).start()

            spread(ref, array, line, 2).start()

        @pl.when(zz + step < depth)
        def _():
            line = zz + step
            settle(block(ref, line * 2 + yy), tok_z.at[array, line])

            @pl.when(zz > 0)
            def _():
                spread(ref, array, line, 1).start()

            spread(ref, array, line, 2).start()

    ahead = depth - 1
    exchange(0)
    acc[...] = jnp.zeros_like(acc)
    part[...] = jnp.zeros_like(part)
    stage_out.wait()
    for step in range(1, depth):
        relay(tok_v, 0, step)
        if step < ahead:
            exchange(step)

    def lane_pick(values, lane):
        ids = lax.broadcasted_iota(jnp.int32, values.shape, 1)
        return jnp.sum(jnp.where(ids == lane, values, 0.0), axis=1, keepdims=True)

    tiles = outer * count // TILE

    def gate_up(j):
        slot = j % 2
        settle(gu_v.at[slot], load_sem.at[slot])
        for e in range(PAIR):
            def tile(m, carry, e=e):
                at = pl.ds(pl.multiple_of(m * TILE, TILE), TILE)
                weights = gu_v[slot, e].reshape(devices * rows, 2 * LANES)
                h = jnp.dot(tok_v[at, :], weights, preferred_element_type=jnp.float32)
                g, u = h[:, :LANES], h[:, LANES:]
                a = g / (1.0 + jnp.exp(-g)) * u
                act[j % RING, at, e * LANES:(e + 1) * LANES] = a.astype(jnp.bfloat16)
                return carry

            lax.fori_loop(0, tiles, tile, 0)

    def load_down(j):
        for k in range(inner):
            there = (i + k) % inner
            source = wdn.at[pl.ds(j * PAIR, PAIR)] if k == 0 else dn.at[pl.ds(j * PAIR, PAIR), there]
            pltpu.make_async_copy(source, dn_v.at[j % 2, :, there], dn_sem.at[j % 2]).start()

    def down(j, carry):
        slot = j % 2
        settle(dn_v.at[slot], dn_sem.at[slot])

        @pl.when(j + 1 < chunks)
        def _():
            load_down(j + 1)

        def tile(m, carry):
            at = pl.ds(pl.multiple_of(m * TILE, TILE), TILE)
            weights = dn_v[slot].reshape(PAIR * inner * hidden, width)
            v = lax.dot_general(
                cot_v[at, :width], weights, (((1,), (1,)), ((), ())),
                preferred_element_type=jnp.float32,
            )
            gates = cot_v[at, width:].astype(jnp.float32)
            ids = lax.broadcasted_iota(jnp.int32, gates.shape, 1)
            sums = part[at, :]
            scaled = []
            for e in range(PAIR):
                a = act[j % RING, at, e * LANES:(e + 1) * LANES].astype(jnp.float32)
                total = jnp.sum(a * v[:, e * LANES:(e + 1) * LANES], axis=1, keepdims=True)
                sums = jnp.where(ids == j * PAIR + e, total, sums)
                scaled.append((a * lane_pick(gates, j * PAIR + e)).astype(jnp.bfloat16))
            part[at, :] = sums
            lhs = jnp.concatenate(scaled, axis=1)
            acc[at, :] += jnp.dot(lhs, weights, preferred_element_type=jnp.float32)
            return carry

        lax.fori_loop(0, tiles, tile, 0)
        return carry

    def step(q, carry):
        @pl.when(q < depth - 1)
        def _():
            relay(cot_v, 1, q + 1)

        @pl.when(q + ahead < chunks)
        def _():
            exchange(q + ahead)

        for r in range(outer):
            origin = (o + outer - r) % outer
            piece = gu.at[pl.ds(q * PAIR, PAIR), origin * chips + xx, c]
            if r:
                settle(piece, a2a_r.at[q, r])
            for k in range(1, chips):
                remote(piece, piece, x_s.at[k], x_r.at[q, k], x_peer(k)).start()

        @pl.when(q == 0)
        def _():
            for k in range(1, chips):
                there = ((xx + chips - k) % chips) * 2 + c
                settle(dn.at[:, there], dn_xr.at[k])
                remote(dn.at[:, there], dn.at[:, there], dn_ps.at[k], dn_pr.at[k], partner).start()

        @pl.when(q == 1)
        def _():
            pltpu.make_async_copy(tok, tok_v.at[own_rows], loc_sem.at[0]).wait()
            for line in range(depth):
                settle(block(tok_v, line * 2 + (1 - yy)), tok_y.at[0, line])

        @pl.when(q >= 1)
        def _():
            gate_up(q - 1)

        for k in range(1, chips):
            settle(gu.at[pl.ds(0, PAIR), pl.ds(0, outer), 0], x_r.at[q, k])
        mine = gu.at[pl.ds(q * PAIR, PAIR), :, c]
        remote(mine, mine, p_s, p_r.at[q], partner).start()

        @pl.when(q == depth - 1)
        def _():
            pltpu.make_async_copy(cot, cot_v.at[own_rows], loc_sem.at[1]).wait()
            for line in range(depth):
                settle(block(cot_v, line * 2 + (1 - yy)), tok_y.at[1, line])
            for k in range(chips):
                settle(dn.at[:, 0], dn_pr.at[k])
            load_down(0)

        begin = jnp.where(q < depth - 1, 0, jnp.minimum(2 * (q - depth + 1), q - 1))
        end = jnp.where(q < depth - 1, 0, jnp.minimum(2 * (q - depth + 1) + 2, q))
        lax.fori_loop(begin, end, down, 0)

        settle(mine, p_r.at[q])
        pltpu.make_async_copy(
            gu.at[pl.ds(q * PAIR, PAIR)], gu_v.at[q % 2], load_sem.at[q % 2]
        ).start()
        return carry

    lax.fori_loop(0, chunks, step, 0)
    gate_up(chunks - 1)
    down(chunks - 1, 0)

    for ref, array, source in arrays:
        for line in range(depth):
            @pl.when((zz < depth - 1) & (line <= zz))
            def _(ref=ref, array=array, line=line):
                spread(ref, array, line, 0).wait_send()

            @pl.when((zz > 0) & (line >= zz))
            def _(ref=ref, array=array, line=line):
                spread(ref, array, line, 1).wait_send()

            spread(ref, array, line, 2).wait_send()

    turned = part[...].T[:experts]
    for b in range(outer):
        part_out[b] = turned[:, b * count:(b + 1) * count]
    for r in range(1, outer):
        remote(
            part_out.at[(o + r) % outer], part_in.at[r], gr_s.at[r], gr_r.at[r], group_peer(r)
        ).start()

    def sum_at(line):
        return acc[pl.ds(pl.multiple_of((line * 2 + yy) * count, count), count), :]

    def y_send(line):
        there = pl.ds(pl.multiple_of((line * 2 + (1 - yy)) * count, count), count)
        slot = pl.ds(pl.multiple_of(line * count, count), count)
        tok_v[slot, :] = acc[there, :].astype(jnp.bfloat16)
        remote(tok_v.at[slot], y_in.at[line], ry_s.at[line], ry_r.at[line], y_peer).start()

    def z_send(line, direction, more):
        slot_at = depth + jnp.where(line < zz, line, line - 1)
        slot = pl.ds(pl.multiple_of(slot_at * count, count), count)
        settle(y_in.at[line], ry_r.at[line])
        total = sum_at(line) + y_in[line].astype(jnp.float32)

        @pl.when(more)
        def _():
            settle(z_in.at[direction, line], rz_r.at[direction, line])
            tok_v[slot, :] = (total + z_in[direction, line].astype(jnp.float32)).astype(jnp.bfloat16)

        @pl.when(jnp.logical_not(more))
        def _():
            tok_v[slot, :] = total.astype(jnp.bfloat16)

        remote(
            tok_v.at[slot], z_in.at[direction, line], rz_s.at[line], rz_r.at[direction, line],
            (right, left)[direction],
        ).start()

    for far in range(depth - 1, 0, -1):
        @pl.when(zz + far < depth)
        def _(far=far):
            y_send(zz + far)

        @pl.when(zz >= far)
        def _(far=far):
            y_send(zz - far)
    y_send(zz)
    for far in range(depth - 1, 0, -1):
        @pl.when(zz + far < depth)
        def _(far=far):
            z_send(zz + far, 0, zz > 0)

        @pl.when(zz >= far)
        def _(far=far):
            z_send(zz - far, 1, zz < depth - 1)
    settle(y_in.at[zz], ry_r.at[zz])
    own = pl.ds(pl.multiple_of(o * count, count), count)
    acc[own, :] += y_in[zz].astype(jnp.float32)

    @pl.when(zz > 0)
    def _():
        settle(z_in.at[0, zz], rz_r.at[0, zz])
        acc[own, :] += z_in[0, zz].astype(jnp.float32)

    @pl.when(zz < depth - 1)
    def _():
        settle(z_in.at[1, zz], rz_r.at[1, zz])
        acc[own, :] += z_in[1, zz].astype(jnp.float32)

    out[...] = acc[own, :].astype(jnp.bfloat16)
    grads[...] = part_out[o]
    for r in range(1, outer):
        settle(part_in.at[r], gr_r.at[r])
        grads[...] += part_in[r]

    for r in range(1, outer):
        settle(part_in.at[r], gr_s.at[r])
    for line in range(depth):
        settle(y_in.at[line], ry_s.at[line])

        @pl.when(line != zz)
        def _(line=line):
            settle(y_in.at[line], rz_s.at[line])
    settle(wgu.at[pl.ds(0, outer - 1)], a2a_s)
    for k in range(1, chips):
        settle(wgu, x_s.at[k])
        settle(wdn, dn_xs.at[k])
    settle(gu.at[:, :, 0], p_s)
    for k in range(chips):
        settle(wdn, dn_ps.at[k])


def fast(
    tokens, cotangent, routes, gates, previous_row, gu_payload, gu_scales, down_payload, down_scales
):
    count, width = tokens.shape
    experts, rows, _ = gu_payload.shape
    hidden = down_payload.shape[1]
    devices = lax.axis_size("expert")
    hidden_width = gu_payload.shape[2] // 2
    outer = hidden_width // LANES
    inner = devices // outer
    chips, depth = inner // 2, outer // 2
    device_id = lax.axis_index("expert")

    ids = jnp.arange(experts, dtype=jnp.int32)
    row_of = jnp.sum(jnp.where(routes[:, :, None] == ids, previous_row, 0), axis=2)
    hits = row_of[:, :, None] == jnp.arange(LANES, dtype=jnp.int32)
    dense = jnp.sum(jnp.where(hits, gates.astype(jnp.float32)[:, :, None], 0.0), axis=1)
    cot = jnp.concatenate([cotangent, dense.astype(jnp.bfloat16)], axis=1)

    first = device_id * rows // LANES
    second = jnp.minimum(first + 1, gu_scales.shape[1] - 1)
    in_first = ((device_id * rows + jnp.arange(rows)) // LANES == first)[None, :, None]
    low = lax.dynamic_slice_in_dim(gu_scales, first, 1, axis=1)
    high = lax.dynamic_slice_in_dim(gu_scales, second, 1, axis=1)
    scale = jnp.where(in_first, low, high).reshape(experts, rows, 2, outer, 1)
    wgu = gu_payload.reshape(experts, rows, 2, outer, LANES).astype(jnp.float32) * scale
    wgu = wgu.astype(jnp.bfloat16).transpose(3, 0, 1, 2, 4).reshape(outer, experts, rows, 2 * LANES)
    scale = lax.dynamic_slice_in_dim(down_scales, device_id * hidden // LANES, 1, axis=1)
    wdn = down_payload.reshape(experts, hidden, width // LANES, LANES).astype(jnp.float32)
    wdn = (wdn * scale[..., None]).astype(jnp.bfloat16).reshape(experts, hidden, width)

    chunks = experts // PAIR
    group = outer * count
    bf16, f32 = jnp.bfloat16, jnp.float32
    dma = pltpu.SemaphoreType.DMA
    anywhere = pl.BlockSpec(memory_space=pl.ANY)
    vmem = pl.BlockSpec(memory_space=pltpu.VMEM)
    out, grads, _, _ = pl.pallas_call(
        functools.partial(layer_kernel, (outer, inner, count, rows, width)),
        out_shape=[
            jax.ShapeDtypeStruct((count, width), bf16),
            jax.ShapeDtypeStruct((experts, count), f32),
            jax.ShapeDtypeStruct((experts, devices // 2, 2, rows, 2 * LANES), bf16),
            jax.ShapeDtypeStruct((experts, inner, hidden, width), bf16),
        ],
        in_specs=[anywhere] * 4,
        out_specs=[vmem, vmem, anywhere, anywhere],
        scratch_shapes=[
            pltpu.VMEM((group, width), bf16),
            pltpu.VMEM((group, width + LANES), bf16),
            pltpu.VMEM((group, width), f32),
            pltpu.VMEM((RING, group, PAIR * LANES), bf16),
            pltpu.VMEM((2, PAIR, devices // 2, 2, rows, 2 * LANES), bf16),
            pltpu.VMEM((2, PAIR, inner, hidden, width), bf16),
            pltpu.VMEM((experts, rows, 2 * LANES), bf16),
            pltpu.VMEM((depth, count, width), bf16),
            pltpu.VMEM((2, depth, count, width), bf16),
            pltpu.VMEM((group, LANES), f32),
            pltpu.VMEM((outer, experts, count), f32),
            pltpu.VMEM((outer, experts, count), f32),
            dma(()), dma((chunks, outer)),
            dma((chips,)), dma((chunks, chips)),
            dma(()), dma((chunks,)),
            dma(()), dma((2,)), dma((2,)),
            dma((chips,)), dma((chips,)), dma((chips,)), dma((chips,)),
            dma((2, 3, depth)), dma((2, depth)), dma((2, depth)), dma((2,)),
            dma((depth,)), dma((depth,)), dma((depth,)), dma((2, depth)),
            dma((outer,)), dma((outer,)),
        ],
        compiler_params=pltpu.CompilerParams(
            collective_id=0, has_side_effects=True, vmem_limit_bytes=66000000
        ),
    )(wgu, wdn, tokens, cot)
    grads = grads.T
    own = row_of[:, :, None] == ids
    gate_grad = jnp.sum(jnp.where(own, grads[:, None, :], 0.0), axis=2)
    return (out, gate_grad)


def choose(devices, tokens, cotangent, routes, gates, previous_row, gu_payload, *rest):
    down_payload = rest[1]
    if fits(
        devices, gu_payload.shape[0], gu_payload.shape[1], down_payload.shape[1],
        gu_payload.shape[2] // 2,
    ):
        return fast(tokens, cotangent, routes, gates, previous_row, gu_payload, *rest)
    return shards(tokens, cotangent, routes, gates, previous_row, gu_payload, *rest)


def solution(mesh):
    in_specs = (
        P("expert", None),
        P("expert", None),
        P("expert", None),
        P("expert", None),
        P(),
        P(None, "expert", None),
        P(),
        P(None, "expert", None),
        P(),
    )
    out_specs = (P("expert", None), P("expert", None))
    return jax.shard_map(
        functools.partial(choose, mesh.shape["expert"]), mesh=mesh, in_specs=in_specs, out_specs=out_specs, check_vma=False)
```

```python
import functools

import jax
import jax.numpy as jnp
from jax import lax
from jax.experimental import pallas as pl
from jax.experimental.pallas import tpu as pltpu
from jax.sharding import PartitionSpec as P


def dequantize(payload, scales):
    expanded = jnp.repeat(jnp.repeat(scales, 128, axis=0), 128, axis=1)
    return (payload.astype(jnp.float32) * expanded).astype(jnp.bfloat16)


def plan(routes, gates, previous_row, most):
    local_count = routes.shape[0]
    rows = previous_row.shape[0]
    ids = jnp.arange(rows, dtype=jnp.int32)
    row_of = jnp.sum(jnp.where(routes[:, :, None] == ids, previous_row, 0), axis=2)
    hits = row_of[:, :, None] == ids
    chosen = jnp.sum(hits.astype(jnp.float32), axis=1)
    gate_of = jnp.sum(jnp.where(hits, gates.astype(jnp.float32)[:, :, None], 0.0), axis=1)
    places = jnp.arange(local_count, dtype=jnp.int32)
    before = (places[:, None] < places[None, :]).astype(jnp.bfloat16)
    rank = jnp.einsum(
        "ut,us->st", before, chosen.astype(jnp.bfloat16), preferred_element_type=jnp.float32
    ).astype(jnp.int32)
    slots = jnp.arange(most, dtype=jnp.int32)
    picked = (rank[:, None, :] == slots[None, :, None]) & (chosen.T[:, None, :] > 0)
    select = picked.astype(jnp.bfloat16)
    weigh = jnp.where(picked, gate_of.T[:, None, :], 0.0).astype(jnp.bfloat16)
    return hits, select.reshape(rows * most, local_count), weigh.reshape(rows * most, local_count)


def shards(
    tokens, cotangent, routes, gates, previous_row, gu_payload, gu_scales, down_payload, down_scales
):
    local_count, model_width = tokens.shape
    top = routes.shape[1]
    hidden_width = gu_payload.shape[2] // 2
    devices = lax.axis_size("expert")
    device_id = lax.axis_index("expert")
    experts = previous_row.shape[0]
    copies = devices // experts
    groups = [[c * experts + i for i in range(experts)] for c in range(copies)]
    most = local_count * top * 5 // (4 * experts)
    hits, select, weigh = plan(routes, gates, previous_row, most)
    outgoing = jnp.dot(select, tokens, preferred_element_type=jnp.float32).astype(jnp.bfloat16)
    outgoing = outgoing.reshape(experts, most, model_width)
    arrived = lax.all_to_all(
        outgoing, "expert", split_axis=0, concat_axis=0, tiled=True, axis_index_groups=groups
    )
    send_gate = jnp.concatenate([gu_payload] * copies, axis=0)
    send_down = jnp.concatenate([down_payload] * copies, axis=0)
    got_gate = lax.all_to_all(send_gate, "expert", split_axis=0, concat_axis=0, tiled=True)
    got_down = lax.all_to_all(send_down, "expert", split_axis=0, concat_axis=0, tiled=True)
    own_row = device_id % experts
    w_gu = dequantize(got_gate.reshape(model_width, 2 * hidden_width), gu_scales[own_row])
    w_down = dequantize(got_down.reshape(hidden_width, model_width), down_scales[own_row])
    row_block = arrived.reshape(-1, model_width)
    hidden = jnp.dot(row_block, w_gu, preferred_element_type=jnp.float32)
    active = (jax.nn.silu(hidden[:, :hidden_width]) * hidden[:, hidden_width:]).astype(jnp.bfloat16)
    result = jnp.dot(active, w_down, preferred_element_type=jnp.float32).astype(jnp.bfloat16)
    returned = lax.all_to_all(
        result.reshape(arrived.shape),
        "expert",
        split_axis=0,
        concat_axis=0,
        tiled=True,
        axis_index_groups=groups,
    ).reshape(-1, model_width)
    layer_out = jnp.einsum(
        "st,sd->td", weigh, returned, preferred_element_type=jnp.float32
    ).astype(jnp.bfloat16)
    dots = jnp.einsum("sd,td->st", returned, cotangent, preferred_element_type=jnp.float32)
    dots = jnp.sum(
        jnp.where(select > 0, dots, 0.0).reshape(experts, most, local_count), axis=1
    )
    gate_grad = jnp.sum(jnp.where(hits, dots.T[:, None, :], 0.0), axis=2)
    return (layer_out, gate_grad)


LANES = 128
PAIR = 2
AHEAD = 2
CUTS = 8
TILE = 512
MESH = pl.DeviceIdType.MESH


def fits(devices, experts, stored_rows, hidden_rows, hidden_width):
    outer = hidden_width // LANES
    return (
        hidden_width % LANES == 0
        and outer % 2 == 0
        and devices % (2 * outer) == 0
        and experts % PAIR == 0
        and experts >= 8 * PAIR
        and experts <= LANES
        and stored_rows % 16 == 0
        and stored_rows <= LANES
        and hidden_rows % 16 == 0
        and LANES % hidden_rows == 0
    )


def layer_kernel(
    sizes, wgu, wdn, tok, cot,
    out, grads, gu, dn,
    tok_v, cot_v, acc, act, gu_v, dn_v, own_v, y_in, z_in, part, part_out, part_in,
    a2a_s, a2a_r, own_s, own_r, x_s, x_r, p_s, p_r, own_sem, load_sem, dn_sem, dn_xs, dn_xr, dn_ps, dn_pr,
    tok_s, tok_z, tok_y, cot_s, cot_z, cot_y, loc_sem, ry_s, ry_r, rz_s, rz_r, gr_s, gr_r,
):
    outer, inner, count, rows, width = sizes
    chips, depth = inner // 2, outer // 2
    experts = wdn.shape[0]
    hidden = wdn.shape[1]
    chunks = experts // PAIR
    devices = outer * inner
    me = lax.axis_index("expert")
    o, i = me // inner, me % inner
    zz, yy, xx, c = o // 2, o % 2, i // 2, i % 2
    place = o * chips + xx
    partner = o * inner + xx * 2 + (1 - c)
    y_peer = (zz * 2 + (1 - yy)) * inner + i
    right, left = me + 2 * inner, me - 2 * inner

    def group_peer(r):
        return ((o + r) % outer) * inner + i

    def x_peer(k):
        return o * inner + ((xx + k) % chips) * 2 + c

    def remote(src, dst, send, recv, device):
        return pltpu.make_async_remote_copy(
            src_ref=src, dst_ref=dst, send_sem=send, recv_sem=recv,
            device_id=(device,), device_id_type=MESH,
        )

    def settle(ref, sem):
        pltpu.make_async_copy(ref, ref, sem).wait()

    stage_in = pltpu.make_async_copy(wgu.at[o], own_v, own_sem)
    stage_in.start()
    own_rows = pl.ds(pl.multiple_of(o * count, count), count)
    for source, target, slot in ((tok, tok_v, 0), (cot, cot_v, 1)):
        pltpu.make_async_copy(source, target.at[own_rows], loc_sem.at[slot]).start()

    barrier = pltpu.get_barrier_semaphore()
    for r in range(1, outer):
        pl.semaphore_signal(barrier, inc=1, device_id=(group_peer(r),), device_id_type=MESH)
    for k in range(1, chips):
        pl.semaphore_signal(barrier, inc=1, device_id=(x_peer(k),), device_id_type=MESH)
    pl.semaphore_signal(barrier, inc=1, device_id=(partner,), device_id_type=MESH)
    pl.semaphore_wait(barrier, outer + chips - 1)

    def block(ref, index):
        return ref.at[pl.ds(pl.multiple_of(index * count, count), count)]

    def spread(ref, array, line, direction, source=None):
        target = (right, left, y_peer)[direction]
        there = block(ref, line * 2 + yy)
        arrive = tok_y.at[array, line] if direction == 2 else tok_z.at[array, line]
        return remote(
            there if source is None else source, there,
            tok_s.at[array, direction, line], arrive, target,
        )

    def offer(ref, array, source):
        @pl.when(zz < depth - 1)
        def _():
            spread(ref, array, zz, 0, source).start()

        @pl.when(zz > 0)
        def _():
            spread(ref, array, zz, 1, source).start()

        spread(ref, array, zz, 2, source).start()

    offer(tok_v, 0, tok)

    for k in range(1, chips):
        remote(wdn, dn.at[:, i], dn_xs.at[k], dn_xr.at[k], x_peer(k)).start()
    remote(wdn, dn.at[:, i], dn_ps.at[0], dn_pr.at[0], partner).start()

    stage_in.wait()
    stage_out = pltpu.make_async_copy(own_v, gu.at[:, place, c], own_sem)
    stage_out.start()
    for k in range(1, chips):
        piece = gu.at[:, place, c]
        remote(wgu.at[o], piece, own_s.at[k], own_r.at[k], x_peer(k)).start()

    even, odd = tuple(range(2, outer, 2)), tuple(range(1, outer, 2))

    def exchange(q):
        for r in even + odd:
            remote(
                wgu.at[(o + r) % outer, pl.ds(q * PAIR, PAIR)],
                gu.at[pl.ds(q * PAIR, PAIR), place, c],
                a2a_s, a2a_r.at[q, r], group_peer(r),
            ).start()

    def relay(ref, array, step):
        @pl.when(zz >= step)
        def _():
            line = zz - step
            settle(block(ref, line * 2 + yy), tok_z.at[array, line])

            @pl.when(zz < depth - 1)
            def _():
                spread(ref, array, line, 0).start()

            spread(ref, array, line, 2).start()

        @pl.when(zz + step < depth)
        def _():
            line = zz + step
            settle(block(ref, line * 2 + yy), tok_z.at[array, line])

            @pl.when(zz > 0)
            def _():
                spread(ref, array, line, 1).start()

            spread(ref, array, line, 2).start()

    acc[...] = jnp.zeros_like(acc)
    part[...] = jnp.zeros_like(part)
    stage_out.wait()
    for step in range(1, depth):
        relay(tok_v, 0, step)
        if step == depth - 2:
            exchange(0)
    for q in range(1, AHEAD):
        exchange(q)

    def lane_pick(values, lane):
        ids = lax.broadcasted_iota(jnp.int32, values.shape, 1)
        return jnp.sum(jnp.where(ids == lane, values, 0.0), axis=1, keepdims=True)

    tiles = outer * count // TILE

    def gate_up(j):
        slot = j % 2
        settle(gu_v.at[slot], load_sem.at[slot])
        for e in range(PAIR):
            def tile(m, carry, e=e):
                at = pl.ds(pl.multiple_of(m * TILE, TILE), TILE)
                weights = gu_v[slot, e].reshape(devices * rows, 2 * LANES)
                h = jnp.dot(tok_v[at, :width], weights, preferred_element_type=jnp.float32)
                g, u = h[:, :LANES], h[:, LANES:]
                a = g / (1.0 + jnp.exp(-g)) * u
                act[j, at, e * LANES:(e + 1) * LANES] = a.astype(jnp.bfloat16)
                return carry

            lax.fori_loop(0, tiles, tile, 0)

    def load_down(j):
        for k in range(inner):
            there = (i + k) % inner
            source = wdn.at[pl.ds(j * PAIR, PAIR)] if k == 0 else dn.at[pl.ds(j * PAIR, PAIR), there]
            pltpu.make_async_copy(source, dn_v.at[j % 2, :, there], dn_sem.at[j % 2]).start()

    def down_rows(j):
        settle(dn_v.at[j % 2], dn_sem.at[j % 2])

        @pl.when(j + 1 < chunks)
        def _():
            load_down(j + 1)

        return dn_v[j % 2].reshape(PAIR * inner * hidden, width)

    def down(j):
        weights = down_rows(j)

        def tile(m, carry):
            at = pl.ds(pl.multiple_of(m * TILE, TILE), TILE)
            gates = tok_v[at, width:].astype(jnp.float32)
            scaled = []
            for e in range(PAIR):
                a = act[j, at, e * LANES:(e + 1) * LANES].astype(jnp.float32)
                scaled.append((a * lane_pick(gates, j * PAIR + e)).astype(jnp.bfloat16))
            lhs = jnp.concatenate(scaled, axis=1)
            acc[at, :] += jnp.dot(lhs, weights, preferred_element_type=jnp.float32)
            return carry

        lax.fori_loop(0, tiles, tile, 0)

    def gate_sums(j, carry):
        weights = down_rows(j)

        def tile(m, inside):
            at = pl.ds(pl.multiple_of(m * TILE, TILE), TILE)
            v = lax.dot_general(
                cot_v[at, :], weights, (((1,), (1,)), ((), ())),
                preferred_element_type=jnp.float32,
            )
            sums = part[at, :]
            ids = lax.broadcasted_iota(jnp.int32, sums.shape, 1)
            for e in range(PAIR):
                a = act[j, at, e * LANES:(e + 1) * LANES].astype(jnp.float32)
                total = jnp.sum(a * v[:, e * LANES:(e + 1) * LANES], axis=1, keepdims=True)
                sums = jnp.where(ids == j * PAIR + e, total, sums)
            part[at, :] = sums
            return inside

        lax.fori_loop(0, tiles, tile, 0)
        return carry

    cut = count // CUTS

    def cut_at(line, side, n):
        return cot_v.at[pl.ds(pl.multiple_of((line * 2 + side) * count + n * cut, cut), cut)]

    def cut_send(line, direction, n, source=None):
        there = cut_at(line, yy, n)
        arrive = cot_y.at[line] if direction == 2 else cot_z.at[line, n]
        remote(
            there if source is None else source, there, cot_s.at[direction, line], arrive,
            (right, left, y_peer)[direction],
        ).start()

    def cut_relay(line, direction, n):
        settle(cut_at(line, yy, n), cot_z.at[line, n])

        @pl.when((zz < depth - 1) if direction == 0 else (zz > 0))
        def _():
            cut_send(line, direction, n)

        cut_send(line, 2, n)

    def cut_step(t):
        for k in range(1, depth):
            n = t - k

            @pl.when((n >= 0) & (n < CUTS) & (zz >= k))
            def _(n=n, k=k):
                cut_relay(zz - k, 0, n)

            @pl.when((n >= 0) & (n < CUTS) & (zz + k < depth))
            def _(n=n, k=k):
                cut_relay(zz + k, 1, n)

        @pl.when(t < CUTS)
        def _():
            source = cot.at[pl.ds(pl.multiple_of(t * cut, cut), cut)]

            @pl.when(zz < depth - 1)
            def _():
                cut_send(zz, 0, t, source)

            @pl.when(zz > 0)
            def _():
                cut_send(zz, 1, t, source)

            cut_send(zz, 2, t, source)

    def pass_on(q, steps):
        for r in steps:
            origin = (o + outer - r) % outer
            piece = gu.at[pl.ds(q * PAIR, PAIR), origin * chips + xx, c]
            settle(piece, a2a_r.at[q, r])
            for k in range(1, chips):
                remote(piece, piece, x_s.at[k], x_r.at[q, k], x_peer(k)).start()

    def step(t, carry):
        @pl.when(t + AHEAD < chunks)
        def _():
            exchange(t + AHEAD)

        @pl.when(t < chunks)
        def _():
            pass_on(t, even)

        @pl.when(t == 1)
        def _():
            for k in range(1, chips):
                there = ((xx + chips - k) % chips) * 2 + c
                settle(dn.at[:, there], dn_xr.at[k])
                remote(dn.at[:, there], dn.at[:, there], dn_ps.at[k], dn_pr.at[k], partner).start()
                settle(gu.at[:, 0, 0], own_r.at[k])

        @pl.when(t >= 1)
        def _():
            for k in range(1, chips):
                settle(gu.at[pl.ds(0, PAIR), pl.ds(0, outer - 1), 0], x_r.at[t - 1, k])
            mine = gu.at[pl.ds((t - 1) * PAIR, PAIR), :, c]
            remote(mine, mine, p_s, p_r.at[t - 1], partner).start()

        @pl.when(t == 2)
        def _():
            pltpu.make_async_copy(tok, tok_v.at[own_rows], loc_sem.at[0]).wait()
            for line in range(depth):
                settle(block(tok_v, line * 2 + (1 - yy)), tok_y.at[0, line])
            for k in range(chips):
                settle(dn.at[:, 0], dn_pr.at[k])
            load_down(0)

        @pl.when(t >= 2)
        def _():
            gate_up(t - 2)
            down(t - 2)

        @pl.when(t < chunks)
        def _():
            pass_on(t, odd)

        @pl.when(t >= 1)
        def _():
            settle(gu.at[pl.ds(0, PAIR), :, c], p_r.at[t - 1])
            pltpu.make_async_copy(
                gu.at[pl.ds((t - 1) * PAIR, PAIR)], gu_v.at[(t - 1) % 2], load_sem.at[(t - 1) % 2]
            ).start()

        cut_step(t)
        return carry

    lax.fori_loop(0, chunks + 1, step, 0)
    gate_up(chunks - 1)
    cut_step(chunks + 1)
    down(chunks - 1)
    cut_step(chunks + 2)
    load_down(0)

    for ref, array in ((tok_v, 0),):
        for line in range(depth):
            @pl.when((zz < depth - 1) & (line <= zz))
            def _(ref=ref, array=array, line=line):
                spread(ref, array, line, 0).wait_send()

            @pl.when((zz > 0) & (line >= zz))
            def _(ref=ref, array=array, line=line):
                spread(ref, array, line, 1).wait_send()

            spread(ref, array, line, 2).wait_send()

    def sum_at(line):
        return acc[pl.ds(pl.multiple_of((line * 2 + yy) * count, count), count), :]

    def y_send(line):
        there = pl.ds(pl.multiple_of((line * 2 + (1 - yy)) * count, count), count)
        slot = pl.ds(pl.multiple_of(line * count, count), count)
        tok_v[slot, :width] = acc[there, :].astype(jnp.bfloat16)
        remote(tok_v.at[slot, pl.ds(0, width)], y_in.at[line], ry_s.at[line], ry_r.at[line], y_peer).start()

    def z_send(line, direction, more):
        slot_at = depth + jnp.where(line < zz, line, line - 1)
        slot = pl.ds(pl.multiple_of(slot_at * count, count), count)
        settle(y_in.at[line], ry_r.at[line])
        total = sum_at(line) + y_in[line].astype(jnp.float32)

        @pl.when(more)
        def _():
            settle(z_in.at[direction, line], rz_r.at[direction, line])
            tok_v[slot, :width] = (total + z_in[direction, line].astype(jnp.float32)).astype(jnp.bfloat16)

        @pl.when(jnp.logical_not(more))
        def _():
            tok_v[slot, :width] = total.astype(jnp.bfloat16)

        remote(
            tok_v.at[slot, pl.ds(0, width)], z_in.at[direction, line], rz_s.at[line], rz_r.at[direction, line],
            (right, left)[direction],
        ).start()

    for far in range(depth - 1, 0, -1):
        @pl.when(zz + far < depth)
        def _(far=far):
            y_send(zz + far)

        @pl.when(zz >= far)
        def _(far=far):
            y_send(zz - far)
    y_send(zz)
    pltpu.make_async_copy(cot, cot_v.at[own_rows], loc_sem.at[1]).wait()
    for line in range(depth):
        settle(block(cot_v, line * 2 + (1 - yy)), cot_y.at[line])
    lax.fori_loop(0, chunks, gate_sums, 0)
    turned = part[...].T[:experts]
    for b in range(outer):
        part_out[b] = turned[:, b * count:(b + 1) * count]
    for r in range(1, outer):
        remote(
            part_out.at[(o + r) % outer], part_in.at[r], gr_s.at[r], gr_r.at[r], group_peer(r)
        ).start()

    for far in range(depth - 1, 0, -1):
        @pl.when(zz + far < depth)
        def _(far=far):
            z_send(zz + far, 0, zz > 0)

        @pl.when(zz >= far)
        def _(far=far):
            z_send(zz - far, 1, zz < depth - 1)
    settle(y_in.at[zz], ry_r.at[zz])
    own = pl.ds(pl.multiple_of(o * count, count), count)
    acc[own, :] += y_in[zz].astype(jnp.float32)

    @pl.when(zz > 0)
    def _():
        settle(z_in.at[0, zz], rz_r.at[0, zz])
        acc[own, :] += z_in[0, zz].astype(jnp.float32)

    @pl.when(zz < depth - 1)
    def _():
        settle(z_in.at[1, zz], rz_r.at[1, zz])
        acc[own, :] += z_in[1, zz].astype(jnp.float32)

    out[...] = acc[own, :].astype(jnp.bfloat16)
    grads[...] = part_out[o]
    for r in range(1, outer):
        settle(part_in.at[r], gr_r.at[r])
        grads[...] += part_in[r]

    for r in range(1, outer):
        settle(part_in.at[r], gr_s.at[r])
    for line in range(depth):
        settle(y_in.at[line], ry_s.at[line])

        @pl.when(line != zz)
        def _(line=line):
            settle(y_in.at[line], rz_s.at[line])
        @pl.when((zz < depth - 1) & (line <= zz))
        def _(line=line):
            settle(y_in.at[line], cot_s.at[0, line])

        @pl.when((zz > 0) & (line >= zz))
        def _(line=line):
            settle(y_in.at[line], cot_s.at[1, line])

        settle(y_in.at[line], cot_s.at[2, line])
    settle(wgu.at[pl.ds(0, outer - 1)], a2a_s)
    for k in range(1, chips):
        settle(wgu.at[pl.ds(0, outer - 1)], x_s.at[k])
        settle(wgu.at[0], own_s.at[k])
        settle(wdn, dn_xs.at[k])
    settle(gu.at[:, :, 0], p_s)
    for k in range(chips):
        settle(wdn, dn_ps.at[k])


def fast(
    tokens, cotangent, routes, gates, previous_row, gu_payload, gu_scales, down_payload, down_scales
):
    count, width = tokens.shape
    experts, rows, _ = gu_payload.shape
    hidden = down_payload.shape[1]
    devices = lax.axis_size("expert")
    hidden_width = gu_payload.shape[2] // 2
    outer = hidden_width // LANES
    inner = devices // outer
    chips, depth = inner // 2, outer // 2
    device_id = lax.axis_index("expert")

    ids = jnp.arange(experts, dtype=jnp.int32)
    row_of = jnp.sum(jnp.where(routes[:, :, None] == ids, previous_row, 0), axis=2)
    hits = row_of[:, :, None] == jnp.arange(LANES, dtype=jnp.int32)
    dense = jnp.sum(jnp.where(hits, gates.astype(jnp.float32)[:, :, None], 0.0), axis=1)
    tok = jnp.concatenate([tokens, dense.astype(jnp.bfloat16)], axis=1)

    first = device_id * rows // LANES
    second = jnp.minimum(first + 1, gu_scales.shape[1] - 1)
    in_first = ((device_id * rows + jnp.arange(rows)) // LANES == first)[None, :, None]
    low = lax.dynamic_slice_in_dim(gu_scales, first, 1, axis=1)
    high = lax.dynamic_slice_in_dim(gu_scales, second, 1, axis=1)
    scale = jnp.where(in_first, low, high).reshape(experts, rows, 2, outer, 1)
    wgu = gu_payload.reshape(experts, rows, 2, outer, LANES).astype(jnp.float32) * scale
    wgu = wgu.astype(jnp.bfloat16).transpose(3, 0, 1, 2, 4).reshape(outer, experts, rows, 2 * LANES)
    scale = lax.dynamic_slice_in_dim(down_scales, device_id * hidden // LANES, 1, axis=1)
    wdn = down_payload.reshape(experts, hidden, width // LANES, LANES).astype(jnp.float32)
    wdn = (wdn * scale[..., None]).astype(jnp.bfloat16).reshape(experts, hidden, width)

    chunks = experts // PAIR
    group = outer * count
    bf16, f32 = jnp.bfloat16, jnp.float32
    dma = pltpu.SemaphoreType.DMA
    anywhere = pl.BlockSpec(memory_space=pl.ANY)
    vmem = pl.BlockSpec(memory_space=pltpu.VMEM)
    out, grads, _, _ = pl.pallas_call(
        functools.partial(layer_kernel, (outer, inner, count, rows, width)),
        out_shape=[
            jax.ShapeDtypeStruct((count, width), bf16),
            jax.ShapeDtypeStruct((experts, count), f32),
            jax.ShapeDtypeStruct((experts, devices // 2, 2, rows, 2 * LANES), bf16),
            jax.ShapeDtypeStruct((experts, inner, hidden, width), bf16),
        ],
        in_specs=[anywhere] * 4,
        out_specs=[vmem, vmem, anywhere, anywhere],
        scratch_shapes=[
            pltpu.VMEM((group, width + LANES), bf16),
            pltpu.VMEM((group, width), bf16),
            pltpu.VMEM((group, width), f32),
            pltpu.VMEM((chunks, group, PAIR * LANES), bf16),
            pltpu.VMEM((2, PAIR, devices // 2, 2, rows, 2 * LANES), bf16),
            pltpu.VMEM((2, PAIR, inner, hidden, width), bf16),
            pltpu.VMEM((experts, rows, 2 * LANES), bf16),
            pltpu.VMEM((depth, count, width), bf16),
            pltpu.VMEM((2, depth, count, width), bf16),
            pltpu.VMEM((group, LANES), f32),
            pltpu.VMEM((outer, experts, count), f32),
            pltpu.VMEM((outer, experts, count), f32),
            dma(()), dma((chunks, outer)),
            dma((chips,)), dma((chips,)),
            dma((chips,)), dma((chunks, chips)),
            dma(()), dma((chunks,)),
            dma(()), dma((2,)), dma((2,)),
            dma((chips,)), dma((chips,)), dma((chips,)), dma((chips,)),
            dma((1, 3, depth)), dma((1, depth)), dma((1, depth)),
            dma((3, depth)), dma((depth, CUTS)), dma((depth,)), dma((2,)),
            dma((depth,)), dma((depth,)), dma((depth,)), dma((2, depth)),
            dma((outer,)), dma((outer,)),
        ],
        compiler_params=pltpu.CompilerParams(
            collective_id=0, has_side_effects=True, vmem_limit_bytes=66000000
        ),
    )(wgu, wdn, tok, cotangent)
    grads = grads.T
    own = row_of[:, :, None] == ids
    gate_grad = jnp.sum(jnp.where(own, grads[:, None, :], 0.0), axis=2)
    return (out, gate_grad)


def choose(devices, tokens, cotangent, routes, gates, previous_row, gu_payload, *rest):
    down_payload = rest[1]
    if fits(
        devices, gu_payload.shape[0], gu_payload.shape[1], down_payload.shape[1],
        gu_payload.shape[2] // 2,
    ):
        return fast(tokens, cotangent, routes, gates, previous_row, gu_payload, *rest)
    return shards(tokens, cotangent, routes, gates, previous_row, gu_payload, *rest)


def solution(mesh):
    in_specs = (
        P("expert", None),
        P("expert", None),
        P("expert", None),
        P("expert", None),
        P(),
        P(None, "expert", None),
        P(),
        P(None, "expert", None),
        P(),
    )
    out_specs = (P("expert", None), P("expert", None))
    return jax.shard_map(
        functools.partial(choose, mesh.shape["expert"]), mesh=mesh, in_specs=in_specs, out_specs=out_specs, check_vma=False)
```

```python
import functools

import jax
import jax.numpy as jnp
from jax import lax
from jax.experimental import pallas as pl
from jax.experimental.pallas import tpu as pltpu
from jax.sharding import PartitionSpec as P


def dequantize(payload, scales):
    expanded = jnp.repeat(jnp.repeat(scales, 128, axis=0), 128, axis=1)
    return (payload.astype(jnp.float32) * expanded).astype(jnp.bfloat16)


def plan(routes, gates, previous_row, most):
    local_count = routes.shape[0]
    rows = previous_row.shape[0]
    ids = jnp.arange(rows, dtype=jnp.int32)
    row_of = jnp.sum(jnp.where(routes[:, :, None] == ids, previous_row, 0), axis=2)
    hits = row_of[:, :, None] == ids
    chosen = jnp.sum(hits.astype(jnp.float32), axis=1)
    gate_of = jnp.sum(jnp.where(hits, gates.astype(jnp.float32)[:, :, None], 0.0), axis=1)
    places = jnp.arange(local_count, dtype=jnp.int32)
    before = (places[:, None] < places[None, :]).astype(jnp.bfloat16)
    rank = jnp.einsum(
        "ut,us->st", before, chosen.astype(jnp.bfloat16), preferred_element_type=jnp.float32
    ).astype(jnp.int32)
    slots = jnp.arange(most, dtype=jnp.int32)
    picked = (rank[:, None, :] == slots[None, :, None]) & (chosen.T[:, None, :] > 0)
    select = picked.astype(jnp.bfloat16)
    weigh = jnp.where(picked, gate_of.T[:, None, :], 0.0).astype(jnp.bfloat16)
    return hits, select.reshape(rows * most, local_count), weigh.reshape(rows * most, local_count)


def shards(
    tokens, cotangent, routes, gates, previous_row, gu_payload, gu_scales, down_payload, down_scales
):
    local_count, model_width = tokens.shape
    top = routes.shape[1]
    hidden_width = gu_payload.shape[2] // 2
    devices = lax.axis_size("expert")
    device_id = lax.axis_index("expert")
    experts = previous_row.shape[0]
    copies = devices // experts
    groups = [[c * experts + i for i in range(experts)] for c in range(copies)]
    most = local_count * top * 5 // (4 * experts)
    hits, select, weigh = plan(routes, gates, previous_row, most)
    outgoing = jnp.dot(select, tokens, preferred_element_type=jnp.float32).astype(jnp.bfloat16)
    outgoing = outgoing.reshape(experts, most, model_width)
    arrived = lax.all_to_all(
        outgoing, "expert", split_axis=0, concat_axis=0, tiled=True, axis_index_groups=groups
    )
    send_gate = jnp.concatenate([gu_payload] * copies, axis=0)
    send_down = jnp.concatenate([down_payload] * copies, axis=0)
    got_gate = lax.all_to_all(send_gate, "expert", split_axis=0, concat_axis=0, tiled=True)
    got_down = lax.all_to_all(send_down, "expert", split_axis=0, concat_axis=0, tiled=True)
    own_row = device_id % experts
    w_gu = dequantize(got_gate.reshape(model_width, 2 * hidden_width), gu_scales[own_row])
    w_down = dequantize(got_down.reshape(hidden_width, model_width), down_scales[own_row])
    row_block = arrived.reshape(-1, model_width)
    hidden = jnp.dot(row_block, w_gu, preferred_element_type=jnp.float32)
    active = (jax.nn.silu(hidden[:, :hidden_width]) * hidden[:, hidden_width:]).astype(jnp.bfloat16)
    result = jnp.dot(active, w_down, preferred_element_type=jnp.float32).astype(jnp.bfloat16)
    returned = lax.all_to_all(
        result.reshape(arrived.shape),
        "expert",
        split_axis=0,
        concat_axis=0,
        tiled=True,
        axis_index_groups=groups,
    ).reshape(-1, model_width)
    layer_out = jnp.einsum(
        "st,sd->td", weigh, returned, preferred_element_type=jnp.float32
    ).astype(jnp.bfloat16)
    dots = jnp.einsum("sd,td->st", returned, cotangent, preferred_element_type=jnp.float32)
    dots = jnp.sum(
        jnp.where(select > 0, dots, 0.0).reshape(experts, most, local_count), axis=1
    )
    gate_grad = jnp.sum(jnp.where(hits, dots.T[:, None, :], 0.0), axis=2)
    return (layer_out, gate_grad)


LANES = 128
PAIR = 2
AHEAD = 2
CUTS = 8
TILE = 512
MESH = pl.DeviceIdType.MESH


def fits(devices, experts, stored_rows, hidden_rows, hidden_width):
    outer = hidden_width // LANES
    return (
        hidden_width % LANES == 0
        and outer % 2 == 0
        and devices % (2 * outer) == 0
        and experts % PAIR == 0
        and experts >= 8 * PAIR
        and experts == 2 * PAIR * (devices // outer)
        and experts <= LANES
        and stored_rows % 16 == 0
        and stored_rows <= LANES
        and hidden_rows % 16 == 0
        and LANES % hidden_rows == 0
    )


def layer_kernel(
    sizes, gu_raw, dn_raw, gu_scale, dn_scale, tok, dense, cot,
    out, grads, gu, dn, wgu,
    tok_v, cot_v, acc, act, gu_v, dn_v, raw_v, stage, y_in, z_in, part, part_out, part_in,
    a2a_s, a2a_r, own_s, own_r, x_s, x_r, p_s, p_r, raw_sem, put_sem, keep_sem, load_sem, dn_sem, dn_xs, dn_xr, dn_ps, dn_pr,
    tok_s, tok_z, tok_y, cot_s, cot_z, cot_y, loc_sem, ry_s, ry_r, rz_s, rz_r, gr_s, gr_r,
):
    outer, inner, count, rows, width = sizes
    chips, depth = inner // 2, outer // 2
    experts = dn_raw.shape[0]
    hidden = dn_raw.shape[1]
    devices = outer * inner
    me = lax.axis_index("expert")
    o, i = me // inner, me % inner
    zz, yy, xx, c = o // 2, o % 2, i // 2, i % 2
    place = o * chips + xx
    partner = o * inner + xx * 2 + (1 - c)
    y_peer = (zz * 2 + (1 - yy)) * inner + i
    right, left = me + 2 * inner, me - 2 * inner

    def group_peer(r):
        return ((o + r) % outer) * inner + i

    def x_peer(k):
        return o * inner + ((xx + k) % chips) * 2 + c

    def remote(src, dst, send, recv, device):
        return pltpu.make_async_remote_copy(
            src_ref=src, dst_ref=dst, send_sem=send, recv_sem=recv,
            device_id=(device,), device_id_type=MESH,
        )

    def settle(ref, sem):
        pltpu.make_async_copy(ref, ref, sem).wait()

    def fetch(q):
        return pltpu.make_async_copy(
            gu_raw.at[pl.ds(q * PAIR, PAIR)], raw_v.at[q % 2], raw_sem.at[q % 2]
        )

    half = experts // 2
    for e in range(experts):
        target = dn_v.at[e // half, e % half // inner, e % inner]
        pltpu.make_async_copy(dn_raw.at[e], target, dn_sem.at[e // half]).start()
    own_rows = pl.ds(pl.multiple_of(o * count, count), count)
    load_tok = pltpu.make_async_copy(tok, tok_v.at[own_rows, pl.ds(0, width)], loc_sem.at[0])
    load_tok.start()
    load_dense = pltpu.make_async_copy(
        dense, tok_v.at[own_rows, pl.ds(width, LANES)], loc_sem.at[1]
    )
    load_dense.start()
    load_cot = pltpu.make_async_copy(cot, cot_v.at[own_rows], loc_sem.at[2])
    load_cot.start()
    fetch(0).start()
    fetch(1).start()

    barrier = pltpu.get_barrier_semaphore()
    for r in range(1, outer):
        pl.semaphore_signal(barrier, inc=1, device_id=(group_peer(r),), device_id_type=MESH)
    for k in range(1, chips):
        pl.semaphore_signal(barrier, inc=1, device_id=(x_peer(k),), device_id_type=MESH)
    pl.semaphore_signal(barrier, inc=1, device_id=(partner,), device_id_type=MESH)
    load_tok.wait()
    load_dense.wait()
    pl.semaphore_wait(barrier, outer + chips - 1)

    def block(ref, index):
        return ref.at[pl.ds(pl.multiple_of(index * count, count), count)]

    def spread(ref, array, line, direction, source=None):
        target = (right, left, y_peer)[direction]
        there = block(ref, line * 2 + yy)
        arrive = tok_y.at[array, line] if direction == 2 else tok_z.at[array, line]
        return remote(
            there if source is None else source, there,
            tok_s.at[array, direction, line], arrive, target,
        )

    def offer(ref, array, source):
        @pl.when(zz < depth - 1)
        def _():
            spread(ref, array, zz, 0, source).start()

        @pl.when(zz > 0)
        def _():
            spread(ref, array, zz, 1, source).start()

        spread(ref, array, zz, 2, source).start()

    offer(tok_v, 0, None)

    dn_block = me * hidden // LANES
    for part_of in range(2):
        settle(dn_v.at[part_of], dn_sem.at[part_of])

        def scale_down(k, carry, part_of=part_of):
            e, at = k // inner, k % inner
            for cb in range(width // LANES):
                lanes = slice(cb * LANES, (cb + 1) * LANES)
                values = dn_v[part_of, e, at, :, lanes].astype(jnp.float32)
                values = values * dn_scale[part_of * half + k, dn_block, cb]
                dn_v[part_of, e, at, :, lanes] = values.astype(jnp.bfloat16)
            return carry

        lax.fori_loop(0, half, scale_down, 0)
        for k in range(half):
            pltpu.make_async_copy(
                dn_v.at[part_of, k // inner, k % inner], dn.at[part_of * half + k, i],
                dn_sem.at[part_of],
            ).start()
    for part_of in range(2):
        settle(dn_v.at[part_of], dn_sem.at[part_of])
    mine = dn.at[:, i]
    for k in range(1, chips):
        remote(mine, mine, dn_xs.at[k], dn_xr.at[k], x_peer(k)).start()
    remote(mine, mine, dn_ps.at[0], dn_pr.at[0], partner).start()

    first = me * rows // LANES
    second = jnp.minimum(first + 1, gu_scale.shape[1] - 1)
    upper = lax.broadcasted_iota(jnp.int32, (rows, LANES), 0) < (first + 1) * LANES - me * rows

    def scale_up(q, carry):
        slot = q % 2
        settle(raw_v.at[slot], raw_sem.at[slot])

        @pl.when(q >= 2)
        def _():
            settle(stage.at[slot], put_sem.at[slot])
            settle(stage.at[slot, 0], keep_sem.at[slot])

        for e in range(PAIR):
            for cb in range(2 * outer):
                low, high = gu_scale[q * PAIR + e, first, cb], gu_scale[q * PAIR + e, second, cb]
                values = raw_v[slot, e, :, cb * LANES:(cb + 1) * LANES].astype(jnp.float32)
                values = (values * jnp.where(upper, low, high)).astype(jnp.bfloat16)
                side = cb // outer * LANES
                stage[slot, cb % outer, e, :, side:side + LANES] = values

        @pl.when(q + 2 < chunks)
        def _():
            fetch(q + 2).start()

        these = pl.ds(q * PAIR, PAIR)
        pltpu.make_async_copy(stage.at[slot], wgu.at[:, these], put_sem.at[slot]).start()
        pltpu.make_async_copy(stage.at[slot, o], gu.at[these, place, c], keep_sem.at[slot]).start()
        return carry

    chunks = experts // PAIR
    lax.fori_loop(0, chunks, scale_up, 0)
    for slot in range(2):
        settle(stage.at[slot], put_sem.at[slot])
        settle(stage.at[slot, 0], keep_sem.at[slot])
    for k in range(1, chips):
        piece = gu.at[:, place, c]
        remote(wgu.at[o], piece, own_s.at[k], own_r.at[k], x_peer(k)).start()

    even, odd = tuple(range(2, outer, 2)), tuple(range(1, outer, 2))

    def exchange(q):
        for r in even + odd:
            remote(
                wgu.at[(o + r) % outer, pl.ds(q * PAIR, PAIR)],
                gu.at[pl.ds(q * PAIR, PAIR), place, c],
                a2a_s, a2a_r.at[q, r], group_peer(r),
            ).start()

    def relay(ref, array, step):
        @pl.when(zz >= step)
        def _():
            line = zz - step
            settle(block(ref, line * 2 + yy), tok_z.at[array, line])

            @pl.when(zz < depth - 1)
            def _():
                spread(ref, array, line, 0).start()

            spread(ref, array, line, 2).start()

        @pl.when(zz + step < depth)
        def _():
            line = zz + step
            settle(block(ref, line * 2 + yy), tok_z.at[array, line])

            @pl.when(zz > 0)
            def _():
                spread(ref, array, line, 1).start()

            spread(ref, array, line, 2).start()

    acc[...] = jnp.zeros_like(acc)
    part[...] = jnp.zeros_like(part)
    for step in range(1, depth):
        relay(tok_v, 0, step)
        if step == depth - 2:
            exchange(0)
    for q in range(1, AHEAD):
        exchange(q)

    def lane_pick(values, lane):
        ids = lax.broadcasted_iota(jnp.int32, values.shape, 1)
        return jnp.sum(jnp.where(ids == lane, values, 0.0), axis=1, keepdims=True)

    tiles = outer * count // TILE

    def gate_up(j):
        slot = j % 2
        settle(gu_v.at[slot], load_sem.at[slot])
        for e in range(PAIR):
            def tile(m, carry, e=e):
                at = pl.ds(pl.multiple_of(m * TILE, TILE), TILE)
                weights = gu_v[slot, e].reshape(devices * rows, 2 * LANES)
                h = jnp.dot(tok_v[at, :width], weights, preferred_element_type=jnp.float32)
                g, u = h[:, :LANES], h[:, LANES:]
                a = g / (1.0 + jnp.exp(-g)) * u
                act[j, at, e * LANES:(e + 1) * LANES] = a.astype(jnp.bfloat16)
                return carry

            lax.fori_loop(0, tiles, tile, 0)

    def load_down(j):
        pltpu.make_async_copy(
            dn.at[pl.ds(j * PAIR, PAIR)], dn_v.at[j % 2], dn_sem.at[j % 2]
        ).start()

    def down_rows(j):
        settle(dn_v.at[j % 2], dn_sem.at[j % 2])

        @pl.when(j + 1 < chunks)
        def _():
            load_down(j + 1)

        return dn_v[j % 2].reshape(PAIR * inner * hidden, width)

    def down(j):
        weights = down_rows(j)

        def tile(m, carry):
            at = pl.ds(pl.multiple_of(m * TILE, TILE), TILE)
            gates = tok_v[at, width:].astype(jnp.float32)
            scaled = []
            for e in range(PAIR):
                a = act[j, at, e * LANES:(e + 1) * LANES].astype(jnp.float32)
                scaled.append((a * lane_pick(gates, j * PAIR + e)).astype(jnp.bfloat16))
            lhs = jnp.concatenate(scaled, axis=1)
            acc[at, :] += jnp.dot(lhs, weights, preferred_element_type=jnp.float32)
            return carry

        lax.fori_loop(0, tiles, tile, 0)

    def gate_sums(j, carry):
        weights = down_rows(j)

        def tile(m, inside):
            at = pl.ds(pl.multiple_of(m * TILE, TILE), TILE)
            v = lax.dot_general(
                cot_v[at, :], weights, (((1,), (1,)), ((), ())),
                preferred_element_type=jnp.float32,
            )
            sums = part[at, :]
            ids = lax.broadcasted_iota(jnp.int32, sums.shape, 1)
            for e in range(PAIR):
                a = act[j, at, e * LANES:(e + 1) * LANES].astype(jnp.float32)
                total = jnp.sum(a * v[:, e * LANES:(e + 1) * LANES], axis=1, keepdims=True)
                sums = jnp.where(ids == j * PAIR + e, total, sums)
            part[at, :] = sums
            return inside

        lax.fori_loop(0, tiles, tile, 0)
        return carry

    cut = count // CUTS

    def cut_at(line, side, n):
        return cot_v.at[pl.ds(pl.multiple_of((line * 2 + side) * count + n * cut, cut), cut)]

    def cut_send(line, direction, n, source=None):
        there = cut_at(line, yy, n)
        arrive = cot_y.at[line] if direction == 2 else cot_z.at[line, n]
        remote(
            there if source is None else source, there, cot_s.at[direction, line], arrive,
            (right, left, y_peer)[direction],
        ).start()

    def cut_relay(line, direction, n):
        settle(cut_at(line, yy, n), cot_z.at[line, n])

        @pl.when((zz < depth - 1) if direction == 0 else (zz > 0))
        def _():
            cut_send(line, direction, n)

        cut_send(line, 2, n)

    def cut_step(t):
        for k in range(1, depth):
            n = t - k

            @pl.when((n >= 0) & (n < CUTS) & (zz >= k))
            def _(n=n, k=k):
                cut_relay(zz - k, 0, n)

            @pl.when((n >= 0) & (n < CUTS) & (zz + k < depth))
            def _(n=n, k=k):
                cut_relay(zz + k, 1, n)

        @pl.when(t < CUTS)
        def _():
            source = cot.at[pl.ds(pl.multiple_of(t * cut, cut), cut)]

            @pl.when(zz < depth - 1)
            def _():
                cut_send(zz, 0, t, source)

            @pl.when(zz > 0)
            def _():
                cut_send(zz, 1, t, source)

            cut_send(zz, 2, t, source)

    def pass_on(q, steps):
        for r in steps:
            origin = (o + outer - r) % outer
            piece = gu.at[pl.ds(q * PAIR, PAIR), origin * chips + xx, c]
            settle(piece, a2a_r.at[q, r])
            for k in range(1, chips):
                remote(piece, piece, x_s.at[k], x_r.at[q, k], x_peer(k)).start()

    def step(t, carry):
        @pl.when(t + AHEAD < chunks)
        def _():
            exchange(t + AHEAD)

        @pl.when(t < chunks)
        def _():
            pass_on(t, even)

        @pl.when(t == 1)
        def _():
            for k in range(1, chips):
                there = ((xx + chips - k) % chips) * 2 + c
                settle(dn.at[:, there], dn_xr.at[k])
                remote(dn.at[:, there], dn.at[:, there], dn_ps.at[k], dn_pr.at[k], partner).start()
                settle(gu.at[:, 0, 0], own_r.at[k])

        @pl.when(t >= 1)
        def _():
            for k in range(1, chips):
                settle(gu.at[pl.ds(0, PAIR), pl.ds(0, outer - 1), 0], x_r.at[t - 1, k])
            mine = gu.at[pl.ds((t - 1) * PAIR, PAIR), :, c]
            remote(mine, mine, p_s, p_r.at[t - 1], partner).start()

        @pl.when(t == 2)
        def _():
            for line in range(depth):
                settle(block(tok_v, line * 2 + (1 - yy)), tok_y.at[0, line])
            for k in range(chips):
                settle(dn.at[:, 0], dn_pr.at[k])
            load_down(0)

        @pl.when(t >= 2)
        def _():
            gate_up(t - 2)
            down(t - 2)

        @pl.when(t < chunks)
        def _():
            pass_on(t, odd)

        @pl.when(t >= 1)
        def _():
            settle(gu.at[pl.ds(0, PAIR), :, c], p_r.at[t - 1])
            pltpu.make_async_copy(
                gu.at[pl.ds((t - 1) * PAIR, PAIR)], gu_v.at[(t - 1) % 2], load_sem.at[(t - 1) % 2]
            ).start()

        cut_step(t)
        return carry

    lax.fori_loop(0, chunks + 1, step, 0)
    gate_up(chunks - 1)
    cut_step(chunks + 1)
    down(chunks - 1)
    cut_step(chunks + 2)
    load_down(0)

    for ref, array in ((tok_v, 0),):
        for line in range(depth):
            @pl.when((zz < depth - 1) & (line <= zz))
            def _(ref=ref, array=array, line=line):
                spread(ref, array, line, 0).wait_send()

            @pl.when((zz > 0) & (line >= zz))
            def _(ref=ref, array=array, line=line):
                spread(ref, array, line, 1).wait_send()

            spread(ref, array, line, 2).wait_send()

    def sum_at(line):
        return acc[pl.ds(pl.multiple_of((line * 2 + yy) * count, count), count), :]

    def y_send(line):
        there = pl.ds(pl.multiple_of((line * 2 + (1 - yy)) * count, count), count)
        slot = pl.ds(pl.multiple_of(line * count, count), count)
        tok_v[slot, :width] = acc[there, :].astype(jnp.bfloat16)
        remote(tok_v.at[slot, pl.ds(0, width)], y_in.at[line], ry_s.at[line], ry_r.at[line], y_peer).start()

    def z_send(line, direction, more):
        slot_at = depth + jnp.where(line < zz, line, line - 1)
        slot = pl.ds(pl.multiple_of(slot_at * count, count), count)
        settle(y_in.at[line], ry_r.at[line])
        total = sum_at(line) + y_in[line].astype(jnp.float32)

        @pl.when(more)
        def _():
            settle(z_in.at[direction, line - 1 + direction], rz_r.at[direction, line])
            tok_v[slot, :width] = (total + z_in[direction, line - 1 + direction].astype(jnp.float32)).astype(jnp.bfloat16)

        @pl.when(jnp.logical_not(more))
        def _():
            tok_v[slot, :width] = total.astype(jnp.bfloat16)

        remote(
            tok_v.at[slot, pl.ds(0, width)], z_in.at[direction, line - 1 + direction], rz_s.at[line], rz_r.at[direction, line],
            (right, left)[direction],
        ).start()

    for far in range(depth - 1, 0, -1):
        @pl.when(zz + far < depth)
        def _(far=far):
            y_send(zz + far)

        @pl.when(zz >= far)
        def _(far=far):
            y_send(zz - far)
    y_send(zz)
    load_cot.wait()
    for line in range(depth):
        settle(block(cot_v, line * 2 + (1 - yy)), cot_y.at[line])
    lax.fori_loop(0, chunks, gate_sums, 0)
    turned = part[...].T[:experts]
    for b in range(outer):
        part_out[b] = turned[:, b * count:(b + 1) * count]
    for r in range(1, outer):
        remote(
            part_out.at[(o + r) % outer], part_in.at[r], gr_s.at[r], gr_r.at[r], group_peer(r)
        ).start()

    for far in range(depth - 1, 0, -1):
        @pl.when(zz + far < depth)
        def _(far=far):
            z_send(zz + far, 0, zz > 0)

        @pl.when(zz >= far)
        def _(far=far):
            z_send(zz - far, 1, zz < depth - 1)
    settle(y_in.at[zz], ry_r.at[zz])
    own = pl.ds(pl.multiple_of(o * count, count), count)
    acc[own, :] += y_in[zz].astype(jnp.float32)

    @pl.when(zz > 0)
    def _():
        settle(z_in.at[0, zz - 1], rz_r.at[0, zz])
        acc[own, :] += z_in[0, zz - 1].astype(jnp.float32)

    @pl.when(zz < depth - 1)
    def _():
        settle(z_in.at[1, zz], rz_r.at[1, zz])
        acc[own, :] += z_in[1, zz].astype(jnp.float32)

    out[...] = acc[own, :].astype(jnp.bfloat16)
    grads[...] = part_out[o]
    for r in range(1, outer):
        settle(part_in.at[r], gr_r.at[r])
        grads[...] += part_in[r]

    for r in range(1, outer):
        settle(part_in.at[r], gr_s.at[r])
    for line in range(depth):
        settle(y_in.at[line], ry_s.at[line])

        @pl.when(line != zz)
        def _(line=line):
            settle(y_in.at[line], rz_s.at[line])
        @pl.when((zz < depth - 1) & (line <= zz))
        def _(line=line):
            settle(y_in.at[line], cot_s.at[0, line])

        @pl.when((zz > 0) & (line >= zz))
        def _(line=line):
            settle(y_in.at[line], cot_s.at[1, line])

        settle(y_in.at[line], cot_s.at[2, line])
    settle(wgu.at[pl.ds(0, outer - 1)], a2a_s)
    for k in range(1, chips):
        settle(wgu.at[pl.ds(0, outer - 1)], x_s.at[k])
        settle(wgu.at[0], own_s.at[k])
        settle(dn.at[:, 0], dn_xs.at[k])
    settle(gu.at[:, :, 0], p_s)
    for k in range(chips):
        settle(dn.at[:, 0], dn_ps.at[k])


def fast(
    tokens, cotangent, routes, gates, previous_row, gu_payload, gu_scales, down_payload, down_scales
):
    count, width = tokens.shape
    experts, rows, _ = gu_payload.shape
    hidden = down_payload.shape[1]
    devices = lax.axis_size("expert")
    hidden_width = gu_payload.shape[2] // 2
    outer = hidden_width // LANES
    inner = devices // outer
    chips, depth = inner // 2, outer // 2

    ids = jnp.arange(experts, dtype=jnp.int32)
    row_of = jnp.sum(jnp.where(routes[:, :, None] == ids, previous_row, 0), axis=2)
    hits = row_of[:, :, None] == jnp.arange(LANES, dtype=jnp.int32)
    dense = jnp.sum(jnp.where(hits, gates.astype(jnp.float32)[:, :, None], 0.0), axis=1)
    chunks = experts // PAIR
    group = outer * count
    bf16, f32 = jnp.bfloat16, jnp.float32
    dma = pltpu.SemaphoreType.DMA
    anywhere = pl.BlockSpec(memory_space=pl.ANY)
    vmem = pl.BlockSpec(memory_space=pltpu.VMEM)
    smem = pl.BlockSpec(memory_space=pltpu.SMEM)
    out, grads, _, _, _ = pl.pallas_call(
        functools.partial(layer_kernel, (outer, inner, count, rows, width)),
        out_shape=[
            jax.ShapeDtypeStruct((count, width), bf16),
            jax.ShapeDtypeStruct((experts, count), f32),
            jax.ShapeDtypeStruct((experts, devices // 2, 2, rows, 2 * LANES), bf16),
            jax.ShapeDtypeStruct((experts, inner, hidden, width), bf16),
            jax.ShapeDtypeStruct((outer, experts, rows, 2 * LANES), bf16),
        ],
        in_specs=[anywhere, anywhere, smem, smem, anywhere, anywhere, anywhere],
        out_specs=[vmem, vmem, anywhere, anywhere, anywhere],
        scratch_shapes=[
            pltpu.VMEM((group, width + LANES), bf16),
            pltpu.VMEM((group, width), bf16),
            pltpu.VMEM((group, width), f32),
            pltpu.VMEM((chunks, group, PAIR * LANES), bf16),
            pltpu.VMEM((2, PAIR, devices // 2, 2, rows, 2 * LANES), bf16),
            pltpu.VMEM((2, PAIR, inner, hidden, width), bf16),
            pltpu.VMEM((2, PAIR, rows, 2 * hidden_width), bf16),
            pltpu.VMEM((2, outer, PAIR, rows, 2 * LANES), bf16),
            pltpu.VMEM((depth, count, width), bf16),
            pltpu.VMEM((2, depth - 1, count, width), bf16),
            pltpu.VMEM((group, LANES), f32),
            pltpu.VMEM((outer, experts, count), f32),
            pltpu.VMEM((outer, experts, count), f32),
            dma(()), dma((chunks, outer)),
            dma((chips,)), dma((chips,)),
            dma((chips,)), dma((chunks, chips)),
            dma(()), dma((chunks,)),
            dma((2,)), dma((2,)), dma((2,)), dma((2,)), dma((2,)),
            dma((chips,)), dma((chips,)), dma((chips,)), dma((chips,)),
            dma((1, 3, depth)), dma((1, depth)), dma((1, depth)),
            dma((3, depth)), dma((depth, CUTS)), dma((depth,)), dma((3,)),
            dma((depth,)), dma((depth,)), dma((depth,)), dma((2, depth)),
            dma((outer,)), dma((outer,)),
        ],
        compiler_params=pltpu.CompilerParams(
            collective_id=0, has_side_effects=True, vmem_limit_bytes=67000000
        ),
    )(
        gu_payload, down_payload, gu_scales, down_scales, tokens, dense.astype(bf16), cotangent
    )
    grads = grads.T
    own = row_of[:, :, None] == ids
    gate_grad = jnp.sum(jnp.where(own, grads[:, None, :], 0.0), axis=2)
    return (out, gate_grad)


def choose(devices, tokens, cotangent, routes, gates, previous_row, gu_payload, *rest):
    down_payload = rest[1]
    if fits(
        devices, gu_payload.shape[0], gu_payload.shape[1], down_payload.shape[1],
        gu_payload.shape[2] // 2,
    ):
        return fast(tokens, cotangent, routes, gates, previous_row, gu_payload, *rest)
    return shards(tokens, cotangent, routes, gates, previous_row, gu_payload, *rest)


def solution(mesh):
    in_specs = (
        P("expert", None),
        P("expert", None),
        P("expert", None),
        P("expert", None),
        P(),
        P(None, "expert", None),
        P(),
        P(None, "expert", None),
        P(),
    )
    out_specs = (P("expert", None), P("expert", None))
    return jax.shard_map(
        functools.partial(choose, mesh.shape["expert"]), mesh=mesh, in_specs=in_specs, out_specs=out_specs, check_vma=False)
```

```python
import functools

import jax
import jax.numpy as jnp
from jax import lax
from jax.experimental import pallas as pl
from jax.experimental.pallas import tpu as pltpu
from jax.sharding import PartitionSpec as P


def dequantize(payload, scales):
    expanded = jnp.repeat(jnp.repeat(scales, 128, axis=0), 128, axis=1)
    return (payload.astype(jnp.float32) * expanded).astype(jnp.bfloat16)


def plan(routes, gates, previous_row, most):
    local_count = routes.shape[0]
    rows = previous_row.shape[0]
    ids = jnp.arange(rows, dtype=jnp.int32)
    row_of = jnp.sum(jnp.where(routes[:, :, None] == ids, previous_row, 0), axis=2)
    hits = row_of[:, :, None] == ids
    chosen = jnp.sum(hits.astype(jnp.float32), axis=1)
    gate_of = jnp.sum(jnp.where(hits, gates.astype(jnp.float32)[:, :, None], 0.0), axis=1)
    places = jnp.arange(local_count, dtype=jnp.int32)
    before = (places[:, None] < places[None, :]).astype(jnp.bfloat16)
    rank = jnp.einsum(
        "ut,us->st", before, chosen.astype(jnp.bfloat16), preferred_element_type=jnp.float32
    ).astype(jnp.int32)
    slots = jnp.arange(most, dtype=jnp.int32)
    picked = (rank[:, None, :] == slots[None, :, None]) & (chosen.T[:, None, :] > 0)
    select = picked.astype(jnp.bfloat16)
    weigh = jnp.where(picked, gate_of.T[:, None, :], 0.0).astype(jnp.bfloat16)
    return hits, select.reshape(rows * most, local_count), weigh.reshape(rows * most, local_count)


def shards(
    tokens, cotangent, routes, gates, previous_row, gu_payload, gu_scales, down_payload, down_scales
):
    local_count, model_width = tokens.shape
    top = routes.shape[1]
    hidden_width = gu_payload.shape[2] // 2
    devices = lax.axis_size("expert")
    device_id = lax.axis_index("expert")
    experts = previous_row.shape[0]
    copies = devices // experts
    groups = [[c * experts + i for i in range(experts)] for c in range(copies)]
    most = local_count * top * 5 // (4 * experts)
    hits, select, weigh = plan(routes, gates, previous_row, most)
    outgoing = jnp.dot(select, tokens, preferred_element_type=jnp.float32).astype(jnp.bfloat16)
    outgoing = outgoing.reshape(experts, most, model_width)
    arrived = lax.all_to_all(
        outgoing, "expert", split_axis=0, concat_axis=0, tiled=True, axis_index_groups=groups
    )
    send_gate = jnp.concatenate([gu_payload] * copies, axis=0)
    send_down = jnp.concatenate([down_payload] * copies, axis=0)
    got_gate = lax.all_to_all(send_gate, "expert", split_axis=0, concat_axis=0, tiled=True)
    got_down = lax.all_to_all(send_down, "expert", split_axis=0, concat_axis=0, tiled=True)
    own_row = device_id % experts
    w_gu = dequantize(got_gate.reshape(model_width, 2 * hidden_width), gu_scales[own_row])
    w_down = dequantize(got_down.reshape(hidden_width, model_width), down_scales[own_row])
    row_block = arrived.reshape(-1, model_width)
    hidden = jnp.dot(row_block, w_gu, preferred_element_type=jnp.float32)
    active = (jax.nn.silu(hidden[:, :hidden_width]) * hidden[:, hidden_width:]).astype(jnp.bfloat16)
    result = jnp.dot(active, w_down, preferred_element_type=jnp.float32).astype(jnp.bfloat16)
    returned = lax.all_to_all(
        result.reshape(arrived.shape),
        "expert",
        split_axis=0,
        concat_axis=0,
        tiled=True,
        axis_index_groups=groups,
    ).reshape(-1, model_width)
    layer_out = jnp.einsum(
        "st,sd->td", weigh, returned, preferred_element_type=jnp.float32
    ).astype(jnp.bfloat16)
    dots = jnp.einsum("sd,td->st", returned, cotangent, preferred_element_type=jnp.float32)
    dots = jnp.sum(
        jnp.where(select > 0, dots, 0.0).reshape(experts, most, local_count), axis=1
    )
    gate_grad = jnp.sum(jnp.where(hits, dots.T[:, None, :], 0.0), axis=2)
    return (layer_out, gate_grad)


LANES = 128
PAIR = 2
AHEAD = 2
CUTS = 8
TILE = 512
MESH = pl.DeviceIdType.MESH


def fits(devices, experts, stored_rows, hidden_rows, hidden_width):
    outer = hidden_width // LANES
    return (
        hidden_width % LANES == 0
        and outer % 2 == 0
        and devices % (2 * outer) == 0
        and experts % PAIR == 0
        and experts >= 8 * PAIR
        and experts == 2 * PAIR * (devices // outer)
        and experts <= LANES
        and stored_rows % 16 == 0
        and stored_rows <= LANES
        and hidden_rows % 16 == 0
        and LANES % hidden_rows == 0
    )


def layer_kernel(
    sizes, gu_raw, dn_raw, gu_steps, dn_steps, tok, dense, cot,
    out, grads, gu, dn, wgu,
    gu_scale, dn_scale, tok_v, cot_v, acc, act, gu_v, dn_v, raw_v, stage, y_in, z_in, part, part_out, part_in,
    a2a_s, a2a_r, own_s, own_r, x_s, x_r, p_s, p_r, raw_sem, put_sem, keep_sem, load_sem, dn_sem, dn_xs, dn_xr, dn_ps, dn_pr,
    tok_s, tok_z, tok_y, cot_s, cot_z, cot_y, loc_sem, ry_s, ry_r, rz_s, rz_r, gr_s, gr_r,
):
    outer, inner, count, rows, width = sizes
    chips, depth = inner // 2, outer // 2
    experts = dn_raw.shape[0]
    hidden = dn_raw.shape[1]
    devices = outer * inner
    me = lax.axis_index("expert")
    o, i = me // inner, me % inner
    zz, yy, xx, c = o // 2, o % 2, i // 2, i % 2
    place = o * chips + xx
    partner = o * inner + xx * 2 + (1 - c)
    y_peer = (zz * 2 + (1 - yy)) * inner + i
    right, left = me + 2 * inner, me - 2 * inner

    def group_peer(r):
        return ((o + r) % outer) * inner + i

    def x_peer(k):
        return o * inner + ((xx + k) % chips) * 2 + c

    def remote(src, dst, send, recv, device):
        return pltpu.make_async_remote_copy(
            src_ref=src, dst_ref=dst, send_sem=send, recv_sem=recv,
            device_id=(device,), device_id_type=MESH,
        )

    def settle(ref, sem):
        pltpu.make_async_copy(ref, ref, sem).wait()

    def fetch(q):
        return pltpu.make_async_copy(
            gu_raw.at[pl.ds(q * PAIR, PAIR)], raw_v.at[q % 2], raw_sem.at[q % 2]
        )

    half = experts // 2
    for e in range(experts):
        target = dn_v.at[e // half, e % half // inner, e % inner]
        pltpu.make_async_copy(dn_raw.at[e], target, dn_sem.at[e // half]).start()
    own_rows = pl.ds(pl.multiple_of(o * count, count), count)
    load_tok = pltpu.make_async_copy(tok, tok_v.at[own_rows, pl.ds(0, width)], loc_sem.at[0])
    load_tok.start()
    load_dense = pltpu.make_async_copy(
        dense, tok_v.at[own_rows, pl.ds(width, LANES)], loc_sem.at[1]
    )
    load_dense.start()
    load_cot = pltpu.make_async_copy(cot, cot_v.at[own_rows], loc_sem.at[2])
    load_cot.start()
    load_scales = (
        pltpu.make_async_copy(dn_steps, dn_scale, loc_sem.at[3]),
        pltpu.make_async_copy(gu_steps, gu_scale, loc_sem.at[4]),
    )
    for load in load_scales:
        load.start()
    fetch(0).start()
    fetch(1).start()

    barrier = pltpu.get_barrier_semaphore()
    for r in range(1, outer):
        pl.semaphore_signal(barrier, inc=1, device_id=(group_peer(r),), device_id_type=MESH)
    for k in range(1, chips):
        pl.semaphore_signal(barrier, inc=1, device_id=(x_peer(k),), device_id_type=MESH)
    pl.semaphore_signal(barrier, inc=1, device_id=(partner,), device_id_type=MESH)
    load_tok.wait()
    load_dense.wait()
    for load in load_scales:
        load.wait()
    pl.semaphore_wait(barrier, outer + chips - 1)

    def block(ref, index):
        return ref.at[pl.ds(pl.multiple_of(index * count, count), count)]

    def spread(ref, array, line, direction, source=None):
        target = (right, left, y_peer)[direction]
        there = block(ref, line * 2 + yy)
        arrive = tok_y.at[array, line] if direction == 2 else tok_z.at[array, line]
        return remote(
            there if source is None else source, there,
            tok_s.at[array, direction, line], arrive, target,
        )

    def offer(ref, array, source):
        @pl.when(zz < depth - 1)
        def _():
            spread(ref, array, zz, 0, source).start()

        @pl.when(zz > 0)
        def _():
            spread(ref, array, zz, 1, source).start()

        spread(ref, array, zz, 2, source).start()

    offer(tok_v, 0, None)

    def share_down(part_of):
        mine = dn.at[pl.ds(part_of * half, half), i]
        for k in range(1, chips):
            remote(mine, mine, dn_xs.at[k], dn_xr.at[k], x_peer(k)).start()
        remote(mine, mine, dn_ps.at[0], dn_pr.at[0], partner).start()

    dn_block = me * hidden // LANES
    for part_of in range(2):
        settle(dn_v.at[part_of], dn_sem.at[part_of])

        def scale_down(k, carry, part_of=part_of):
            e, at = k // inner, k % inner
            for cb in range(width // LANES):
                lanes = slice(cb * LANES, (cb + 1) * LANES)
                values = dn_v[part_of, e, at, :, lanes].astype(jnp.float32)
                values = values * dn_scale[part_of * half + k, dn_block, cb]
                dn_v[part_of, e, at, :, lanes] = values.astype(jnp.bfloat16)
            return carry

        lax.fori_loop(0, half, scale_down, 0)
        for k in range(half):
            pltpu.make_async_copy(
                dn_v.at[part_of, k // inner, k % inner], dn.at[part_of * half + k, i],
                dn_sem.at[part_of],
            ).start()
        if part_of:
            settle(dn_v.at[0], dn_sem.at[0])
            share_down(0)
    settle(dn_v.at[1], dn_sem.at[1])
    share_down(1)

    first = me * rows // LANES
    second = jnp.minimum(first + 1, gu_scale.shape[1] - 1)
    upper = lax.broadcasted_iota(jnp.int32, (rows, LANES), 0) < (first + 1) * LANES - me * rows

    def scale_up(q, carry):
        slot = q % 2
        settle(raw_v.at[slot], raw_sem.at[slot])

        @pl.when(q >= 2)
        def _():
            settle(stage.at[slot], put_sem.at[slot])
            settle(stage.at[slot, 0], keep_sem.at[slot])

        for e in range(PAIR):
            for cb in range(2 * outer):
                low, high = gu_scale[q * PAIR + e, first, cb], gu_scale[q * PAIR + e, second, cb]
                values = raw_v[slot, e, :, cb * LANES:(cb + 1) * LANES].astype(jnp.float32)
                values = (values * jnp.where(upper, low, high)).astype(jnp.bfloat16)
                side = cb // outer * LANES
                stage[slot, cb % outer, e, :, side:side + LANES] = values

        @pl.when(q + 2 < chunks)
        def _():
            fetch(q + 2).start()

        these = pl.ds(q * PAIR, PAIR)
        pltpu.make_async_copy(stage.at[slot], wgu.at[:, these], put_sem.at[slot]).start()
        pltpu.make_async_copy(stage.at[slot, o], gu.at[these, place, c], keep_sem.at[slot]).start()
        return carry

    chunks = experts // PAIR
    lax.fori_loop(0, chunks, scale_up, 0)
    for slot in range(2):
        settle(stage.at[slot], put_sem.at[slot])
        settle(stage.at[slot, 0], keep_sem.at[slot])
    for k in range(1, chips):
        piece = gu.at[:, place, c]
        remote(wgu.at[o], piece, own_s.at[k], own_r.at[k], x_peer(k)).start()

    even, odd = tuple(range(2, outer, 2)), tuple(range(1, outer, 2))

    def exchange(q):
        for r in even + odd:
            remote(
                wgu.at[(o + r) % outer, pl.ds(q * PAIR, PAIR)],
                gu.at[pl.ds(q * PAIR, PAIR), place, c],
                a2a_s, a2a_r.at[q, r], group_peer(r),
            ).start()

    def relay(ref, array, step):
        @pl.when(zz >= step)
        def _():
            line = zz - step
            settle(block(ref, line * 2 + yy), tok_z.at[array, line])

            @pl.when(zz < depth - 1)
            def _():
                spread(ref, array, line, 0).start()

            spread(ref, array, line, 2).start()

        @pl.when(zz + step < depth)
        def _():
            line = zz + step
            settle(block(ref, line * 2 + yy), tok_z.at[array, line])

            @pl.when(zz > 0)
            def _():
                spread(ref, array, line, 1).start()

            spread(ref, array, line, 2).start()

    acc[...] = jnp.zeros_like(acc)
    part[...] = jnp.zeros_like(part)
    for step in range(1, depth):
        relay(tok_v, 0, step)
        if step == depth - 2:
            exchange(0)
    for q in range(1, AHEAD):
        exchange(q)

    def lane_pick(values, lane):
        ids = lax.broadcasted_iota(jnp.int32, values.shape, 1)
        return jnp.sum(jnp.where(ids == lane, values, 0.0), axis=1, keepdims=True)

    tiles = outer * count // TILE

    def gate_up(j):
        slot = j % 2
        settle(gu_v.at[slot], load_sem.at[slot])
        for e in range(PAIR):
            def tile(m, carry, e=e):
                at = pl.ds(pl.multiple_of(m * TILE, TILE), TILE)
                weights = gu_v[slot, e].reshape(devices * rows, 2 * LANES)
                h = jnp.dot(tok_v[at, :width], weights, preferred_element_type=jnp.float32)
                g, u = h[:, :LANES], h[:, LANES:]
                a = g / (1.0 + jnp.exp(-g)) * u
                act[j, at, e * LANES:(e + 1) * LANES] = a.astype(jnp.bfloat16)
                return carry

            lax.fori_loop(0, tiles, tile, 0)

    def load_down(j):
        pltpu.make_async_copy(
            dn.at[pl.ds(j * PAIR, PAIR)], dn_v.at[j % 2], dn_sem.at[j % 2]
        ).start()

    def down_rows(j):
        settle(dn_v.at[j % 2], dn_sem.at[j % 2])

        @pl.when(j + 1 < chunks)
        def _():
            load_down(j + 1)

        return dn_v[j % 2].reshape(PAIR * inner * hidden, width)

    def down(j):
        weights = down_rows(j)

        def tile(m, carry):
            at = pl.ds(pl.multiple_of(m * TILE, TILE), TILE)
            gates = tok_v[at, width:].astype(jnp.float32)
            scaled = []
            for e in range(PAIR):
                a = act[j, at, e * LANES:(e + 1) * LANES].astype(jnp.float32)
                scaled.append((a * lane_pick(gates, j * PAIR + e)).astype(jnp.bfloat16))
            lhs = jnp.concatenate(scaled, axis=1)
            acc[at, :] += jnp.dot(lhs, weights, preferred_element_type=jnp.float32)
            return carry

        lax.fori_loop(0, tiles, tile, 0)

    def gate_sums(j, carry):
        weights = down_rows(j)

        def tile(m, inside):
            at = pl.ds(pl.multiple_of(m * TILE, TILE), TILE)
            v = lax.dot_general(
                cot_v[at, :], weights, (((1,), (1,)), ((), ())),
                preferred_element_type=jnp.float32,
            )
            sums = part[at, :]
            ids = lax.broadcasted_iota(jnp.int32, sums.shape, 1)
            for e in range(PAIR):
                a = act[j, at, e * LANES:(e + 1) * LANES].astype(jnp.float32)
                total = jnp.sum(a * v[:, e * LANES:(e + 1) * LANES], axis=1, keepdims=True)
                sums = jnp.where(ids == j * PAIR + e, total, sums)
            part[at, :] = sums
            return inside

        lax.fori_loop(0, tiles, tile, 0)
        return carry

    cut = count // CUTS

    def cut_at(line, side, n):
        return cot_v.at[pl.ds(pl.multiple_of((line * 2 + side) * count + n * cut, cut), cut)]

    def cut_send(line, direction, n, source=None):
        there = cut_at(line, yy, n)
        arrive = cot_y.at[line] if direction == 2 else cot_z.at[line, n]
        remote(
            there if source is None else source, there, cot_s.at[direction, line], arrive,
            (right, left, y_peer)[direction],
        ).start()

    def cut_relay(line, direction, n):
        settle(cut_at(line, yy, n), cot_z.at[line, n])

        @pl.when((zz < depth - 1) if direction == 0 else (zz > 0))
        def _():
            cut_send(line, direction, n)

        cut_send(line, 2, n)

    def cut_step(t):
        for k in range(1, depth):
            n = t - k

            @pl.when((n >= 0) & (n < CUTS) & (zz >= k))
            def _(n=n, k=k):
                cut_relay(zz - k, 0, n)

            @pl.when((n >= 0) & (n < CUTS) & (zz + k < depth))
            def _(n=n, k=k):
                cut_relay(zz + k, 1, n)

        @pl.when(t < CUTS)
        def _():
            source = cot.at[pl.ds(pl.multiple_of(t * cut, cut), cut)]

            @pl.when(zz < depth - 1)
            def _():
                cut_send(zz, 0, t, source)

            @pl.when(zz > 0)
            def _():
                cut_send(zz, 1, t, source)

            cut_send(zz, 2, t, source)

    def pass_on(q, steps):
        for r in steps:
            origin = (o + outer - r) % outer
            piece = gu.at[pl.ds(q * PAIR, PAIR), origin * chips + xx, c]
            settle(piece, a2a_r.at[q, r])
            for k in range(1, chips):
                remote(piece, piece, x_s.at[k], x_r.at[q, k], x_peer(k)).start()

    def step(t, carry):
        @pl.when(t < chunks)
        def _():
            pass_on(t, even)

        @pl.when(t + AHEAD < chunks)
        def _():
            exchange(t + AHEAD)

        @pl.when(t == 1)
        def _():
            for k in range(1, chips):
                there = ((xx + chips - k) % chips) * 2 + c
                settle(dn.at[:, there], dn_xr.at[k])
                remote(dn.at[:, there], dn.at[:, there], dn_ps.at[k], dn_pr.at[k], partner).start()
                settle(gu.at[:, 0, 0], own_r.at[k])

        @pl.when(t >= 1)
        def _():
            for k in range(1, chips):
                settle(gu.at[pl.ds(0, PAIR), pl.ds(0, outer - 1), 0], x_r.at[t - 1, k])
            mine = gu.at[pl.ds((t - 1) * PAIR, PAIR), :, c]
            remote(mine, mine, p_s, p_r.at[t - 1], partner).start()

        @pl.when(t == 2)
        def _():
            for line in range(depth):
                settle(block(tok_v, line * 2 + (1 - yy)), tok_y.at[0, line])
            for k in range(chips):
                settle(dn.at[:, 0], dn_pr.at[k])
            load_down(0)

        @pl.when(t >= 2)
        def _():
            gate_up(t - 2)
            down(t - 2)

        @pl.when(t < chunks)
        def _():
            pass_on(t, odd)

        @pl.when(t >= 1)
        def _():
            settle(gu.at[pl.ds(0, PAIR), :, c], p_r.at[t - 1])
            pltpu.make_async_copy(
                gu.at[pl.ds((t - 1) * PAIR, PAIR)], gu_v.at[(t - 1) % 2], load_sem.at[(t - 1) % 2]
            ).start()

        cut_step(t)
        return carry

    lax.fori_loop(0, chunks + 1, step, 0)
    gate_up(chunks - 1)
    cut_step(chunks + 1)
    down(chunks - 1)
    cut_step(chunks + 2)
    load_down(0)

    for ref, array in ((tok_v, 0),):
        for line in range(depth):
            @pl.when((zz < depth - 1) & (line <= zz))
            def _(ref=ref, array=array, line=line):
                spread(ref, array, line, 0).wait_send()

            @pl.when((zz > 0) & (line >= zz))
            def _(ref=ref, array=array, line=line):
                spread(ref, array, line, 1).wait_send()

            spread(ref, array, line, 2).wait_send()

    def sum_at(line):
        return acc[pl.ds(pl.multiple_of((line * 2 + yy) * count, count), count), :]

    def y_send(line):
        there = pl.ds(pl.multiple_of((line * 2 + (1 - yy)) * count, count), count)
        slot = pl.ds(pl.multiple_of(line * count, count), count)
        tok_v[slot, :width] = acc[there, :].astype(jnp.bfloat16)
        remote(tok_v.at[slot, pl.ds(0, width)], y_in.at[line], ry_s.at[line], ry_r.at[line], y_peer).start()

    def z_send(line, direction, more):
        slot_at = depth + jnp.where(line < zz, line, line - 1)
        slot = pl.ds(pl.multiple_of(slot_at * count, count), count)
        settle(y_in.at[line], ry_r.at[line])
        total = sum_at(line) + y_in[line].astype(jnp.float32)

        @pl.when(more)
        def _():
            settle(z_in.at[direction, line - 1 + direction], rz_r.at[direction, line])
            tok_v[slot, :width] = (total + z_in[direction, line - 1 + direction].astype(jnp.float32)).astype(jnp.bfloat16)

        @pl.when(jnp.logical_not(more))
        def _():
            tok_v[slot, :width] = total.astype(jnp.bfloat16)

        remote(
            tok_v.at[slot, pl.ds(0, width)], z_in.at[direction, line - 1 + direction], rz_s.at[line], rz_r.at[direction, line],
            (right, left)[direction],
        ).start()

    for far in range(depth - 1, 0, -1):
        @pl.when(zz + far < depth)
        def _(far=far):
            y_send(zz + far)

        @pl.when(zz >= far)
        def _(far=far):
            y_send(zz - far)
    y_send(zz)
    load_cot.wait()
    for line in range(depth):
        settle(block(cot_v, line * 2 + (1 - yy)), cot_y.at[line])
    lax.fori_loop(0, chunks, gate_sums, 0)
    turned = part[...].T[:experts]
    for b in range(outer):
        part_out[b] = turned[:, b * count:(b + 1) * count]
    for r in range(1, outer):
        remote(
            part_out.at[(o + r) % outer], part_in.at[r], gr_s.at[r], gr_r.at[r], group_peer(r)
        ).start()

    for far in range(depth - 1, 0, -1):
        @pl.when(zz + far < depth)
        def _(far=far):
            z_send(zz + far, 0, zz > 0)

        @pl.when(zz >= far)
        def _(far=far):
            z_send(zz - far, 1, zz < depth - 1)
    settle(y_in.at[zz], ry_r.at[zz])
    own = pl.ds(pl.multiple_of(o * count, count), count)
    acc[own, :] += y_in[zz].astype(jnp.float32)

    @pl.when(zz > 0)
    def _():
        settle(z_in.at[0, zz - 1], rz_r.at[0, zz])
        acc[own, :] += z_in[0, zz - 1].astype(jnp.float32)

    @pl.when(zz < depth - 1)
    def _():
        settle(z_in.at[1, zz], rz_r.at[1, zz])
        acc[own, :] += z_in[1, zz].astype(jnp.float32)

    out[...] = acc[own, :].astype(jnp.bfloat16)
    grads[...] = part_out[o]
    for r in range(1, outer):
        settle(part_in.at[r], gr_r.at[r])
        grads[...] += part_in[r]

    for r in range(1, outer):
        settle(part_in.at[r], gr_s.at[r])
    for line in range(depth):
        settle(y_in.at[line], ry_s.at[line])

        @pl.when(line != zz)
        def _(line=line):
            settle(y_in.at[line], rz_s.at[line])
        @pl.when((zz < depth - 1) & (line <= zz))
        def _(line=line):
            settle(y_in.at[line], cot_s.at[0, line])

        @pl.when((zz > 0) & (line >= zz))
        def _(line=line):
            settle(y_in.at[line], cot_s.at[1, line])

        settle(y_in.at[line], cot_s.at[2, line])
    settle(wgu.at[pl.ds(0, outer - 1)], a2a_s)
    for k in range(1, chips):
        settle(wgu.at[pl.ds(0, outer - 1)], x_s.at[k])
        settle(wgu.at[0], own_s.at[k])
        settle(dn.at[:, 0], dn_xs.at[k])
    settle(gu.at[:, :, 0], p_s)
    for k in range(chips):
        settle(dn.at[:, 0], dn_ps.at[k])


def fast(
    tokens, cotangent, routes, gates, previous_row, gu_payload, gu_scales, down_payload, down_scales
):
    count, width = tokens.shape
    experts, rows, _ = gu_payload.shape
    hidden = down_payload.shape[1]
    devices = lax.axis_size("expert")
    hidden_width = gu_payload.shape[2] // 2
    outer = hidden_width // LANES
    inner = devices // outer
    chips, depth = inner // 2, outer // 2

    ids = jnp.arange(experts, dtype=jnp.int32)
    row_of = jnp.sum(jnp.where(routes[:, :, None] == ids, previous_row, 0), axis=2)
    hits = row_of[:, :, None] == jnp.arange(LANES, dtype=jnp.int32)
    dense = jnp.sum(jnp.where(hits, gates.astype(jnp.float32)[:, :, None], 0.0), axis=1)
    chunks = experts // PAIR
    group = outer * count
    bf16, f32 = jnp.bfloat16, jnp.float32
    dma = pltpu.SemaphoreType.DMA
    anywhere = pl.BlockSpec(memory_space=pl.ANY)
    vmem = pl.BlockSpec(memory_space=pltpu.VMEM)
    out, grads, _, _, _ = pl.pallas_call(
        functools.partial(layer_kernel, (outer, inner, count, rows, width)),
        out_shape=[
            jax.ShapeDtypeStruct((count, width), bf16),
            jax.ShapeDtypeStruct((experts, count), f32),
            jax.ShapeDtypeStruct((experts, devices // 2, 2, rows, 2 * LANES), bf16),
            jax.ShapeDtypeStruct((experts, inner, hidden, width), bf16),
            jax.ShapeDtypeStruct((outer, experts, rows, 2 * LANES), bf16),
        ],
        in_specs=[anywhere, anywhere, anywhere, anywhere, anywhere, anywhere, anywhere],
        out_specs=[vmem, vmem, anywhere, anywhere, anywhere],
        scratch_shapes=[
            pltpu.SMEM(gu_scales.shape, f32),
            pltpu.SMEM(down_scales.shape, f32),
            pltpu.VMEM((group, width + LANES), bf16),
            pltpu.VMEM((group, width), bf16),
            pltpu.VMEM((group, width), f32),
            pltpu.VMEM((chunks, group, PAIR * LANES), bf16),
            pltpu.VMEM((2, PAIR, devices // 2, 2, rows, 2 * LANES), bf16),
            pltpu.VMEM((2, PAIR, inner, hidden, width), bf16),
            pltpu.VMEM((2, PAIR, rows, 2 * hidden_width), bf16),
            pltpu.VMEM((2, outer, PAIR, rows, 2 * LANES), bf16),
            pltpu.VMEM((depth, count, width), bf16),
            pltpu.VMEM((2, depth - 1, count, width), bf16),
            pltpu.VMEM((group, LANES), f32),
            pltpu.VMEM((outer, experts, count), f32),
            pltpu.VMEM((outer, experts, count), f32),
            dma(()), dma((chunks, outer)),
            dma((chips,)), dma((chips,)),
            dma((chips,)), dma((chunks, chips)),
            dma(()), dma((chunks,)),
            dma((2,)), dma((2,)), dma((2,)), dma((2,)), dma((2,)),
            dma((chips,)), dma((chips,)), dma((chips,)), dma((chips,)),
            dma((1, 3, depth)), dma((1, depth)), dma((1, depth)),
            dma((3, depth)), dma((depth, CUTS)), dma((depth,)), dma((5,)),
            dma((depth,)), dma((depth,)), dma((depth,)), dma((2, depth)),
            dma((outer,)), dma((outer,)),
        ],
        compiler_params=pltpu.CompilerParams(
            collective_id=0, has_side_effects=True, vmem_limit_bytes=67000000
        ),
    )(
        gu_payload, down_payload, gu_scales, down_scales, tokens, dense.astype(bf16), cotangent
    )
    grads = grads.T
    own = row_of[:, :, None] == ids
    gate_grad = jnp.sum(jnp.where(own, grads[:, None, :], 0.0), axis=2)
    return (out, gate_grad)


def choose(devices, tokens, cotangent, routes, gates, previous_row, gu_payload, *rest):
    down_payload = rest[1]
    if fits(
        devices, gu_payload.shape[0], gu_payload.shape[1], down_payload.shape[1],
        gu_payload.shape[2] // 2,
    ):
        return fast(tokens, cotangent, routes, gates, previous_row, gu_payload, *rest)
    return shards(tokens, cotangent, routes, gates, previous_row, gu_payload, *rest)


def solution(mesh):
    in_specs = (
        P("expert", None),
        P("expert", None),
        P("expert", None),
        P("expert", None),
        P(),
        P(None, "expert", None),
        P(),
        P(None, "expert", None),
        P(),
    )
    out_specs = (P("expert", None), P("expert", None))
    return jax.shard_map(
        functools.partial(choose, mesh.shape["expert"]), mesh=mesh, in_specs=in_specs, out_specs=out_specs, check_vma=False)
```
